32 devices in a mesh: band: 4 (over x, core), fld: 8 (over z, y).
Axes of the slice: x: 2, y: 2, z: 4, core: 2. Of those that a mesh axis runs over, the one named last changes fastest.
Arguments:
- spectra: float32 [480, 32, 961], P('fld'), may hold values from -0.006 to 0.006
- pair_slot: int32 [480], replicated, may hold values from 0 to 479, each once
- land_column: int32 [32, 1920], P(('band', 'fld')), may hold values from 0 to 2047, as said below
- owner_map: int32 [32, 1920], P(('band', 'fld')), may hold values from 0 to 7, as said below
- owner_slot: int32 [32, 640], P(('band', 'fld')), may hold values from 0 to 1919, as said below
- state_start: float32 [16, 32, 1920], P(None, ('band', 'fld')), may hold values from -6 to 6
- targets: float32 [16, 32, 1920], P(None, ('band', 'fld')), may hold values from -6 to 6
- amplitudes: float32 [16], replicated, may hold values from -3 to 3
- weight_in: float32 [256, 33], replicated, may hold values from -1 to 1
- weight_out: float32 [16, 256], replicated, may hold values from -0.375 to 0.375
Outputs:
- final_state: float32 [16, 20480], P(None, ('band', 'fld'))
- param_grad: float32 [16, 20480], P(None, ('band', 'fld'))
- amplitude_grad: float32 [16], replicated
The draws below stay inside these ranges and needn't reach their ends.
Inputs may be any that keep to these rules, and one draw needn't show every extreme that they name: `land_column`: within each row the 1920 entries are distinct. owner_map[r, j] = (owner_map[r, 0] + j) mod 8, so that owner_map[r, j] * 240 + j // 8 are distinct within a row. A row has from 1 to 1920 land cells, at its first columns; the counts of a band sum to 5120, one row of every band has 1920, and owner_map[r, 0] is a band's offset plus the land cells of the band's earlier rows, modulo 8. `owner_slot`: the entries of one device are distinct and each names a land cell of its band that owner_map sends to it; every device takes exactly 640 cells, and one row of every band sends 240 cells to every device of the band.
All inputs are finite; a program needn't handle non-finite values.
Results may differ from the reference program's by a relative error of at most 0.0003.
Values sent between devices are 32-bit elements; how exact they have to be, the bound alone decides.
No kernel may reach another device: no remote copies, remote signals or barrier semaphores. Data moves between devices by JAX's collectives and lax.ppermute only.
A program may use at most 64 MiB of HBM per device.

```python
import math
import jax
import jax.numpy as jnp
from jax import lax

FIELDS = 16
STATE = 16
UNITS = 256
WAVES = 960
LONS = 2048
LATS = 1024
STEPS = 4
ROW_MEAN = 640
BANDS = 4
BAND_ROWS = 8
ROWS = 32
PAIRS = 480
COEFS = 961
ROW_MAX = 1920
SEND_CAP = 240
CELLS = 20480


def land_layout(key):
    base_key = jax.random.fold_in(key, 11)
    key_order, key_jitter, key_rotation = jax.random.split(base_key, 3)
    order = jax.vmap(lambda sub_key: jax.random.permutation(sub_key, BAND_ROWS))(jax.random.split(key_order, BANDS))
    position = jnp.arange(BAND_ROWS)
    base_count = jnp.where(position == 0, 3 * ROW_MEAN, jnp.where(position <= 4, ROW_MEAN // 2, ROW_MEAN)).astype(jnp.int32)
    jitter = jax.random.randint(key_jitter, (BANDS, BAND_ROWS - 1), 0, ROW_MEAN // 4 + 1)
    shift_counts = jitter - jnp.roll(jitter, 1, axis=1)
    in_order = base_count[None, :] + jnp.concatenate([jnp.zeros((BANDS, 1), jnp.int32), shift_counts], axis=1)
    counts = jnp.zeros((BANDS, BAND_ROWS), jnp.int32).at[jnp.arange(BANDS)[:, None], order].set(in_order)
    earlier = jnp.cumsum(counts, axis=1) - counts
    rotation = jax.random.randint(key_rotation, (BANDS,), 0, BAND_ROWS)
    cell_index = jnp.arange(ROW_MAX)
    owner_map = (earlier[:, :, None] + cell_index[None, None, :] + rotation[:, None, None]) % BAND_ROWS
    residue = (jnp.arange(BAND_ROWS)[None, :] - rotation[:, None]) % BAND_ROWS
    global_cell = jnp.arange(ROW_MEAN)[None, None, :] * BAND_ROWS + residue[:, :, None]
    source_row = jnp.sum((earlier[:, None, None, :] <= global_cell[:, :, :, None]).astype(jnp.int32), axis=-1) - 1
    start_cell = jnp.take_along_axis(earlier, source_row.reshape(BANDS, BAND_ROWS * ROW_MEAN), axis=1).reshape(BANDS, BAND_ROWS, ROW_MEAN)
    owner_slot = source_row * SEND_CAP + (global_cell - start_cell) // BAND_ROWS
    return (owner_map.reshape(ROWS, ROW_MAX).astype(jnp.int32), owner_slot.reshape(ROWS, ROW_MEAN).astype(jnp.int32))


def draw_owner_map(key, part):
    return land_layout(key)[0]


def draw_owner_slot(key, part):
    return land_layout(key)[1]


def draw_land_column(key, part):
    row_keys = jax.random.split(jax.random.fold_in(key, 5), ROWS)
    return jax.vmap(lambda row_key: jax.random.permutation(row_key, LONS)[:ROW_MAX])(row_keys).astype(jnp.int32)


def steps_of(key, shape, pieces, low, high):
    def one(dim, shards_of):
        heights = jax.random.uniform(jax.random.fold_in(jax.random.fold_in(key, 6), dim), (shards_of,), jnp.float32, low / len(pieces), high / len(pieces))
        return jnp.repeat(jnp.exp(heights), shape[dim] // shards_of).reshape((-1,) + (1,) * (len(shape) - dim - 1))

    level = one(*pieces[0])
    for cut in pieces[1:]:
        level = level * one(*cut)
    return level


def bell_draw(key, extent, deviation, reach, shards=(), dtype=jnp.bfloat16):
    drawn = deviation * jax.random.normal(key, extent, jnp.float32)
    if shards:
        drawn = drawn * steps_of(key, extent, shards, -0.22, 0.18)
    return jnp.clip(drawn, -reach, reach).astype(dtype)


def setup_inputs(seed: int = 0) -> dict:
    seeds = jax.random.split(jax.random.key(seed), 11)
    spectra = bell_draw(seeds[0], (PAIRS, 2 * FIELDS, COEFS), 0.001, 0.006, ((0, 8),), jnp.float32)
    pair_slot = jax.random.permutation(seeds[1], PAIRS).astype(jnp.int32)
    land_column = draw_land_column(jax.random.fold_in(seeds[10], 71), 0)
    owner_map = draw_owner_map(jax.random.fold_in(seeds[10], 71), 0)
    owner_slot = draw_owner_slot(jax.random.fold_in(seeds[10], 71), 0)
    state_start = bell_draw(seeds[5], (STATE, ROWS, ROW_MAX), 1.0, 6.0, ((1, 32),), jnp.float32)
    targets = bell_draw(seeds[6], (STATE, ROWS, ROW_MAX), 1.0, 6.0, ((1, 32),), jnp.float32)
    amplitudes = bell_draw(seeds[7], (FIELDS,), 1.0, 3.0, (), jnp.float32)
    weight_in = bell_draw(seeds[8], (UNITS, STATE + FIELDS + 1), (STATE + FIELDS + 1) ** -0.5, 1.0, (), jnp.float32)
    weight_out = bell_draw(seeds[9], (STATE, UNITS), UNITS ** -0.5, 0.375, (), jnp.float32)
    return dict(spectra=spectra, pair_slot=pair_slot, land_column=land_column, owner_map=owner_map, owner_slot=owner_slot, state_start=state_start, targets=targets, amplitudes=amplitudes, weight_in=weight_in, weight_out=weight_out)


time_step = 0.25

def surrogate_run(pattern, start, target, forcing, amplitudes, weight_in, weight_out):
    highest = lax.Precision.HIGHEST
    params = amplitudes[:, None] * pattern
    state_rows = start.shape[0]

    def hidden_at(state, hour_at):
        joined = jnp.concatenate([state, params, forcing[hour_at][None, :]], axis=0)
        return jnp.tanh(jnp.dot(weight_in, joined, precision=highest))
    states = [start]
    for hour_at in range(STEPS):
        hidden = hidden_at(states[-1], hour_at)
        states.append(states[-1] + time_step * jnp.dot(weight_out, hidden, precision=highest))
    adjoint = states[-1] - target
    param_grad = jnp.zeros_like(params)
    for hour_at in reversed(range(STEPS)):
        hidden = hidden_at(states[hour_at], hour_at)
        through = jnp.dot(weight_out.T, time_step * adjoint, precision=highest) * (1.0 - hidden * hidden)
        joined_grad = jnp.dot(weight_in.T, through, precision=highest)
        adjoint = adjoint + joined_grad[:state_rows]
        param_grad = param_grad + joined_grad[state_rows:state_rows + params.shape[0]]
    return (states[-1], param_grad)

def reference(spectra, pair_slot, land_column, owner_map, owner_slot, state_start, targets, amplitudes, weight_in, weight_out):
    highest = lax.Precision.HIGHEST
    column = jnp.arange(COEFS)
    row_index = jnp.arange(ROWS)

    def pair_terms(packed):
        spec_pair, pair_number = packed
        first_part = column < WAVES - pair_number
        degree = jnp.where(first_part, pair_number + column, column - 1)
        wave_number = jnp.where(first_part, pair_number, WAVES - 1 - pair_number)
        use_sine = wave_number % 2 == 1
        phases = degree[:, None] * (2 * row_index + 1)[None, :] % (4 * LATS)
        angles = phases.astype(jnp.float32) * (math.pi / (2 * LATS))
        basis_table = jnp.where(use_sine[:, None], jnp.sin(angles), jnp.cos(angles))
        first_sum = jnp.dot(jnp.where(first_part[None, :], spec_pair, 0.0), basis_table, precision=highest)
        second_sum = jnp.dot(jnp.where(first_part[None, :], 0.0, spec_pair), basis_table, precision=highest)
        return jnp.stack([first_sum, second_sum])
    fourier = lax.map(pair_terms, (spectra, pair_slot)).reshape(WAVES, 2 * FIELDS, ROWS)
    all_waves = jnp.stack([pair_slot, WAVES - 1 - pair_slot], axis=1).reshape(WAVES)
    by_wave = jnp.zeros((WAVES, 2 * FIELDS, ROWS), jnp.float32).at[all_waves].set(fourier)
    real_part = jnp.transpose(by_wave[:, :FIELDS], (2, 1, 0))
    imag_part = jnp.transpose(by_wave[:, FIELDS:], (2, 1, 0))
    spectrum = lax.complex(real_part, imag_part)
    spectrum = jnp.pad(spectrum, ((0, 0), (0, 0), (0, LONS // 2 + 1 - WAVES)))
    grid = (jnp.fft.irfft(spectrum, n=LONS, axis=-1) * LONS).astype(jnp.float32)
    pattern = grid[row_index[:, None, None], jnp.arange(FIELDS)[None, :, None], land_column[:, None, :]]
    sin_colat = jnp.sin((2 * row_index + 1).astype(jnp.float32) * (math.pi / (2 * LATS)))
    hour_turns = (land_column[:, None, :] * 24 + jnp.arange(STEPS)[None, :, None] * LONS) % (24 * LONS)
    forcing = jnp.maximum(jnp.cos(hour_turns.astype(jnp.float32) * (2.0 * math.pi / (24 * LONS))), 0.0) * sin_colat[:, None, None]
    payload = jnp.concatenate([pattern, jnp.transpose(state_start, (1, 0, 2)), jnp.transpose(targets, (1, 0, 2)), forcing], axis=1)
    send_place = owner_map * SEND_CAP + (jnp.arange(ROW_MAX) // BAND_ROWS)[None, :]
    outbound = jax.vmap(lambda loaded, places: jnp.zeros_like(loaded).at[:, places].set(loaded))(payload, send_place)
    device = jnp.arange(ROWS)[:, None]
    source_rows = device // BAND_ROWS * BAND_ROWS + owner_slot // SEND_CAP
    source_cols = device % BAND_ROWS * SEND_CAP + owner_slot % SEND_CAP
    owned = jnp.transpose(outbound[source_rows, :, source_cols], (0, 2, 1))

    def device_cells(owned_cells):
        owned_pattern = owned_cells[:FIELDS]
        final_state, param_grad = surrogate_run(owned_pattern, owned_cells[FIELDS:FIELDS + STATE], owned_cells[FIELDS + STATE:FIELDS + 2 * STATE], owned_cells[FIELDS + 2 * STATE:], amplitudes, weight_in, weight_out)
        return (final_state, param_grad, lax.optimization_barrier(jnp.sum(param_grad * owned_pattern, axis=1)))
    finals, grads, partials = lax.map(device_cells, owned)
    final_state = jnp.transpose(finals, (1, 0, 2)).reshape(STATE, CELLS)
    param_grad = jnp.transpose(grads, (1, 0, 2)).reshape(FIELDS, CELLS)
    amplitude_grad = lax.optimization_barrier(jnp.sum(partials, axis=0)) / math.sqrt(CELLS)
    return (final_state, param_grad, amplitude_grad)
```

```python
import math

import jax
import jax.numpy as jnp
from jax import lax
from jax.sharding import PartitionSpec as P

FIELDS = 16
STATE = 16
WAVES = 960
LONS = 2048
LATS = 1024
STEPS = 4
ROW_MEAN = 640
COEFS = 961
ROW_MAX = 1920


time_step = 0.25


def surrogate_run(pattern, start, target, forcing, amplitudes, weight_in, weight_out):
    highest = lax.Precision.HIGHEST
    params = amplitudes[:, None] * pattern
    state_rows = start.shape[0]

    def hidden_at(state, hour_at):
        joined = jnp.concatenate([state, params, forcing[hour_at][None, :]], axis=0)
        return jnp.tanh(jnp.dot(weight_in, joined, precision=highest))

    states = [start]
    for hour_at in range(STEPS):
        hidden = hidden_at(states[-1], hour_at)
        states.append(states[-1] + time_step * jnp.dot(weight_out, hidden, precision=highest))
    adjoint = states[-1] - target
    param_grad = jnp.zeros_like(params)
    for hour_at in reversed(range(STEPS)):
        hidden = hidden_at(states[hour_at], hour_at)
        through = jnp.dot(weight_out.T, time_step * adjoint, precision=highest) * (
            1.0 - hidden * hidden
        )
        joined_grad = jnp.dot(weight_in.T, through, precision=highest)
        adjoint = adjoint + joined_grad[:state_rows]
        param_grad = param_grad + joined_grad[state_rows : state_rows + params.shape[0]]
    return (states[-1], param_grad)


def body(
    spectra,
    pair_slot,
    land_column,
    owner_map,
    owner_slot,
    state_start,
    targets,
    amplitudes,
    weight_in,
    weight_out,
):
    highest = lax.Precision.HIGHEST
    band_rows = lax.axis_size("fld")
    band_index = lax.axis_index("band")
    field_index = lax.axis_index("fld")
    pair_count = spectra.shape[0]
    send_cap = ROW_MAX // band_rows
    my_pairs = lax.dynamic_slice_in_dim(pair_slot, field_index * pair_count, pair_count)
    column = jnp.arange(COEFS)
    first_part = column[None, :] < WAVES - my_pairs[:, None]
    degree = jnp.where(first_part, my_pairs[:, None] + column[None, :], column[None, :] - 1)
    wave_number = jnp.where(first_part, my_pairs[:, None], WAVES - 1 - my_pairs[:, None])
    use_sine = wave_number % 2 == 1
    rows_global = band_index * band_rows + jnp.arange(band_rows)
    phases = degree[:, :, None] * (2 * rows_global + 1)[None, None, :] % (4 * LATS)
    angles = phases.astype(jnp.float32) * (math.pi / (2 * LATS))
    basis_table = jnp.where(use_sine[:, :, None], jnp.sin(angles), jnp.cos(angles))
    split_spec = jnp.stack(
        [
            jnp.where(first_part[:, None, :], spectra, 0.0),
            jnp.where(first_part[:, None, :], 0.0, spectra),
        ],
        axis=1,
    )
    fourier = jnp.einsum("swgc,scj->jgsw", split_spec, basis_table, precision=highest)
    fourier = fourier.reshape(band_rows, 2, FIELDS, 2 * pair_count)
    all_waves = jnp.stack([pair_slot, WAVES - 1 - pair_slot], axis=1).reshape(WAVES)
    wave_weight = jnp.where(all_waves == 0, 1.0, 2.0).astype(jnp.float32)
    lon_span = min(256, LONS)
    arrived = lax.all_to_all(fourier, "fld", split_axis=0, concat_axis=3, tiled=True)
    lat_rows, pair_parts, field_count, wave_count = arrived.shape
    coeff_rows = jnp.transpose(arrived, (0, 2, 1, 3)).reshape(
        lat_rows * field_count, pair_parts * wave_count
    )

    def one_block(first_lon):
        longitude = first_lon + jnp.arange(lon_span)
        turns = all_waves[:, None] * longitude[None, :] % LONS
        radians = turns.astype(jnp.float32) * (2.0 * math.pi / LONS)
        dft_table = jnp.concatenate(
            [wave_weight[:, None] * jnp.cos(radians), -wave_weight[:, None] * jnp.sin(radians)],
            axis=0,
        )
        return jnp.dot(coeff_rows, dft_table, precision=highest)

    pieces = lax.map(one_block, jnp.arange(LONS // lon_span) * lon_span)
    grid_row = jnp.transpose(pieces, (1, 0, 2)).reshape(lat_rows, field_count, LONS)[0]
    pattern = grid_row[:, land_column[0]]
    row_number = band_index * band_rows + field_index
    sin_colat = jnp.sin((2 * row_number + 1).astype(jnp.float32) * (math.pi / (2 * LATS)))
    hour_turns = (land_column[0][None, :] * 24 + jnp.arange(STEPS)[:, None] * LONS) % (24 * LONS)
    forcing = (
        jnp.maximum(jnp.cos(hour_turns.astype(jnp.float32) * (2.0 * math.pi / (24 * LONS))), 0.0)
        * sin_colat
    )
    send_place = owner_map[0] * send_cap + jnp.arange(ROW_MAX) // band_rows
    row_state, row_grad = surrogate_run(
        pattern, state_start[:, 0], targets[:, 0], forcing, amplitudes, weight_in, weight_out
    )
    results = jnp.concatenate([row_state, row_grad, row_grad * pattern], axis=0)
    outbound = jnp.zeros_like(results).at[:, send_place].set(results)
    received = lax.all_to_all(outbound, "fld", split_axis=1, concat_axis=1, tiled=True)
    owned = received[:, owner_slot[0]]
    final_state = owned[:STATE]
    param_grad = owned[STATE : STATE + FIELDS]
    partial_value = jnp.sum(owned[STATE + FIELDS :], axis=1)
    device_count = lax.axis_size("band") * band_rows
    copies = jnp.broadcast_to(partial_value[None, :], (device_count, FIELDS))
    partials = lax.all_to_all(copies, ("band", "fld"), split_axis=0, concat_axis=0, tiled=True)
    summed = jnp.sum(partials, axis=0)
    cell_total = lax.axis_size("band") * band_rows * ROW_MEAN
    return (final_state, param_grad, summed / math.sqrt(cell_total))


def solution(mesh):
    return jax.shard_map(
        body,
        mesh=mesh,
        in_specs=(
            P("fld", None, None),
            P(),
            P(("band", "fld"), None),
            P(("band", "fld"), None),
            P(("band", "fld"), None),
            P(None, ("band", "fld"), None),
            P(None, ("band", "fld"), None),
            P(),
            P(),
            P(),
        ),
        out_specs=(P(None, ("band", "fld")), P(None, ("band", "fld")), P()),
        check_vma=False,
    )
```

```python
import functools
import math

import jax
import jax.numpy as jnp
from jax import lax
from jax.experimental import pallas as pl
from jax.experimental.pallas import tpu as pltpu
from jax.sharding import PartitionSpec as P

FIELDS = 16
STATE = 16
UNITS = 256
WAVES = 960
LONS = 2048
LATS = 1024
STEPS = 4
ROW_MEAN = 640
COEFS = 961
ROW_MAX = 1920
PAIRS = 480
TIME_STEP = 0.25

LANES = 128
HALF = LANES // 2
COUNT_LANE = HALF - 1
COEF_PAD = 1024
LON_OUTER = LONS // LANES
WAVE_INNER = 16
VMEM_LIMIT = 60 * 1024 * 1024

f32 = jnp.float32
bf16 = jnp.bfloat16


def iota(shape, dim):
    return lax.broadcasted_iota(jnp.int32, shape, dim)


def sincos_turns(turns):
    part = turns - jnp.round(turns)
    quarter = jnp.round(4.0 * part)
    x = (part - 0.25 * quarter) * (2.0 * math.pi)
    y = x * x
    sine = x * (1.0 + y * (-1.0 / 6 + y * (1.0 / 120 + y * (-1.0 / 5040 + y * (1.0 / 362880)))))
    cosine = 1.0 + y * (-0.5 + y * (1.0 / 24 + y * (-1.0 / 720 + y * (1.0 / 40320))))
    swap = jnp.abs(quarter) == 1.0
    low_sine = jnp.where(swap, cosine, sine)
    low_cosine = jnp.where(swap, sine, cosine)
    sine_flip = (quarter == -1.0) | (jnp.abs(quarter) == 2.0)
    cosine_flip = (quarter == 1.0) | (jnp.abs(quarter) == 2.0)
    return jnp.where(sine_flip, -low_sine, low_sine), jnp.where(cosine_flip, -low_cosine, low_cosine)


def halves(x):
    high = x.astype(bf16)
    return high, (x - high.astype(f32)).astype(bf16)


def dot(a, b):
    return jnp.dot(a, b, preferred_element_type=f32)


def dot_last(a, b):
    return lax.dot_general(a, b, (((1,), (1,)), ((), ())), preferred_element_type=f32)


def pick(pieces, piece_at, lane_at, rows):
    count, load = pieces
    lane_full = jnp.broadcast_to(lane_at, (rows, LANES))
    total = None
    for i in range(count):
        got = jnp.take_along_axis(load(i), lane_full, axis=1)
        total = got if total is None else jnp.where(piece_at == i, got, total)
    return total


def fourier_kernel(nb, pc, cap, gc, pairs_ref, slot_ref, spec_ref, out_ref, tab, ab, thr, lhs):
    step = pl.program_id(0)
    lane = iota((nb, LANES), 1)

    @pl.when(step == 0)
    def _():
        band = lax.axis_index("band")
        first = lax.axis_index("fld") * pc
        odd = (2 * (band * nb + iota((nb, LANES), 0)) + 1).astype(f32) * (1.0 / (4 * LATS))
        for t in range(COEF_PAD // LANES):
            column = (lane + t * LANES).astype(f32)
            for part in range(2):
                sine, cosine = sincos_turns((column - part) * odd)
                high, low = halves(jnp.concatenate([cosine, sine], axis=0))
                for copy in range(2):
                    at = pl.ds(copy * COEF_PAD + t * LANES, LANES)
                    tab[part, 0 : 2 * nb, at] = high
                    tab[part, 2 * nb : 4 * nb, at] = low
        thr[...] = jnp.zeros_like(thr)
        row = jnp.zeros((nb, LANES), f32)
        for s in range(pc):
            pair = pairs_ref[first + s]
            row = jnp.where(lane % HALF == s, pair.astype(f32), row)
            thr[s : s + 1, :] = jnp.full((1, LANES), WAVES - pair, jnp.int32)
        sine, cosine = sincos_turns(row * odd)
        is_odd = row - 2.0 * jnp.floor(row * 0.5) == 1.0
        ab[0] = jnp.where(is_odd, sine, cosine)
        ab[1] = jnp.where(is_odd, cosine, -sine)
        ab[2] = jnp.where(is_odd, 1.0, 0.0)
        lhs[...] = jnp.zeros_like(lhs)

    for t in range(COEF_PAD // LANES):
        width = min(LANES, COEFS - t * LANES)
        first_part = (iota((pc, LANES), 1) + t * LANES < thr[:pc, :])[:, :width]
        for g in range(gc):
            x = spec_ref[:, g, pl.ds(t * LANES, width)]
            high = x.astype(bf16).astype(f32)
            low = x - high
            for k, value in enumerate((high, low)):
                at = pl.ds(k * COEF_PAD + t * LANES, width)
                lhs[0, g * HALF : g * HALF + pc, at] = jnp.where(first_part, value, 0.0).astype(bf16)
                lhs[1, g * HALF : g * HALF + pc, at] = jnp.where(first_part, 0.0, value).astype(bf16)
    sums = []
    for part in range(2):
        both = dot_last(tab[part], lhs[part])
        sums.append(both[: 2 * nb] + both[2 * nb :])
    alpha, beta, is_odd = ab[0], ab[1], ab[2] > 0.0
    low_half = lane < HALF
    for i in range(gc // 2):
        at = slice(i * LANES, (i + 1) * LANES)
        wave0 = alpha * sums[0][:nb, at] + beta * sums[0][nb:, at]
        wave1 = jnp.where(is_odd, sums[1][:nb, at], sums[1][nb:, at])
        out_ref[:, 2 * i, :] = jnp.where(low_half, wave0, pltpu.roll(wave1, HALF, 1))
        out_ref[:, 2 * i + 1, :] = jnp.where(low_half, pltpu.roll(wave0, HALF, 1), wave1)

    @pl.when(step == 0)
    def _():
        slot = jnp.broadcast_to(slot_ref[...], (nb, slot_ref.shape[1]))
        below = iota((nb, slot_ref.shape[1]), 0) * cap
        count = jnp.sum(jnp.where((slot >= below) & (slot < below + cap), 1.0, 0.0), axis=1, keepdims=True)
        out_ref[:, 0, :] = jnp.where(lane == COUNT_LANE, count, out_ref[:, 0, :])


def fourier_call(nb, pc, cap, pair_slot, owner_slot, spectra):
    gc = 8
    return pl.pallas_call(
        functools.partial(fourier_kernel, nb, pc, cap, gc),
        grid=(2 * FIELDS // gc,),
        in_specs=[
            pl.BlockSpec(memory_space=pltpu.SMEM),
            pl.BlockSpec(owner_slot.shape, lambda i: (0, 0)),
            pl.BlockSpec((pc, gc, COEFS), lambda i: (0, i, 0)),
        ],
        out_specs=pl.BlockSpec((nb, gc, LANES), lambda i: (0, i, 0)),
        out_shape=jax.ShapeDtypeStruct((nb, 2 * FIELDS, LANES), f32),
        scratch_shapes=[
            pltpu.VMEM((2, 4 * nb, 2 * COEF_PAD), bf16),
            pltpu.VMEM((3, nb, LANES), f32),
            pltpu.VMEM((HALF, LANES), jnp.int32),
            pltpu.VMEM((2, gc * HALF, 2 * COEF_PAD), bf16),
        ],
        compiler_params=pltpu.CompilerParams(vmem_limit_bytes=VMEM_LIMIT),
        name="fourier",
    )(pair_slot, owner_slot, spectra)


def prepare_kernel(nb, pc, cp, pairs_ref, land_ref, state_ref, target_ref, amp_ref, win_ref, wout_ref,
                   cells_ref, place_ref, inverse_ref, dft_ref, turn_ref, amps_ref,
                   wx_ref, wo_ref, wt_ref, wb_ref):
    lane = iota((1, LANES), 1)
    source_pieces = ROW_MAX // LANES
    row = lax.axis_index("band") * nb + lax.axis_index("fld")
    odd = (2 * row + 1).astype(f32) * (0.5 / (2 * LATS))
    sin_colat = sincos_turns(jnp.full((8, LANES), 1.0, f32) * odd)[0]
    joined = 2 * STATE
    for m in range(nb):
        for q in range(cp // LANES):
            source = nb * (q * LANES + lane) + m
            first = nb * q
            count = min(nb, source_pieces - first)
            at = pl.ds(m * cp + q * LANES, LANES)
            piece_at, lane_at = source // LANES - first, source % LANES

            def load(ref, i):
                return ref[:, 0, pl.ds((first + i) * LANES, LANES)]

            for k, ref in enumerate((state_ref, target_ref)):
                cells_ref[k * STATE : (k + 1) * STATE, at] = pick(
                    (count, functools.partial(load, ref)), piece_at, lane_at, STATE
                )

            def load_land(i):
                return jnp.broadcast_to(land_ref[:, pl.ds((first + i) * LANES, LANES)], (8, LANES))

            column = pick((count, load_land), piece_at, lane_at, 8)
            hour = iota((8, LANES), 0).astype(f32)
            turns = column.astype(f32) * (1.0 / LONS) + hour * (1.0 / 24.0)
            forcing = jnp.maximum(sincos_turns(turns)[1], 0.0) * sin_colat
            place_ref[:, at] = jnp.where(iota((8, LANES), 0) < STEPS, forcing, column.astype(f32))
    for q in range(WAVE_INNER // 2):
        natural = lane + q * LANES
        wave = (natural % HALF) * WAVE_INNER + natural // HALF
        pair = jnp.minimum(wave, WAVES - 1 - wave)
        total = jnp.zeros((8, LANES), jnp.int32)
        rows = iota((8, LANES), 0)
        for i in range(PAIRS // 8):
            here = i * 8 + rows
            arrives = here + ((here.astype(f32) + 0.5) * (1.0 / pc)).astype(jnp.int32) * (LANES - pc)
            total = total + jnp.where(pairs_ref[i * 8 : i * 8 + 8, :] == pair, arrives, 0)
        found = jnp.sum(total.astype(f32), axis=0, keepdims=True).astype(jnp.int32)
        inverse_ref[:, pl.ds(q * LANES, LANES)] = jnp.broadcast_to(
            found + jnp.where(wave >= PAIRS, HALF, 0), (8, LANES)
        )
    a = iota((HALF, LANES), 0)
    sine, cosine = sincos_turns((a * iota((HALF, LANES), 1)).astype(f32) * (1.0 / LANES))
    table = jnp.concatenate(
        [jnp.concatenate([cosine, sine], axis=1), jnp.concatenate([-sine, cosine], axis=1)], axis=0
    )
    high, low = halves(table)
    dft_ref[0:LANES, :] = high
    dft_ref[LANES : 2 * LANES, :] = high
    dft_ref[2 * LANES : 3 * LANES, :] = low
    b = iota((WAVE_INNER, LANES), 0)
    sine, cosine = sincos_turns((b * iota((WAVE_INNER, LANES), 1)).astype(f32) * (1.0 / LONS))
    turn_ref[0:WAVE_INNER, :] = cosine
    turn_ref[WAVE_INNER : 2 * WAVE_INNER, :] = sine
    amp = jnp.broadcast_to(amp_ref[...], (FIELDS, FIELDS))
    diagonal = iota((FIELDS, FIELDS), 0) == iota((FIELDS, FIELDS), 1)
    amps_ref[...] = jnp.broadcast_to(
        jnp.sum(jnp.where(diagonal, amp, 0.0), axis=1, keepdims=True), (FIELDS, LANES)
    )
    win = win_ref[...]
    wout = wout_ref[...]
    high, low = halves(win)
    s, p = slice(0, STATE), slice(STATE, joined)
    tail = jnp.where(iota((UNITS, STATE), 1) == 0, high[:, joined:].astype(f32), 0.0)
    tail = jnp.where(iota((UNITS, STATE), 1) == 1, low[:, joined:].astype(f32), tail)
    tail = jnp.where(iota((UNITS, STATE), 1) == 2, high[:, joined:].astype(f32), tail)
    hf, lf = high.astype(f32), low.astype(f32)
    wx_ref[...] = jnp.concatenate(
        [hf[:, s], lf[:, s], hf[:, s], hf[:, p], lf[:, p], hf[:, p], tail], axis=1
    ).astype(bf16)
    turned = jnp.transpose(win)[:joined]
    high, low = halves(turned)
    wt_ref[0:joined, :] = high
    wt_ref[joined : 2 * joined, :] = low
    high, low = halves(wout)
    wo_ref[0:STATE, :] = high
    wo_ref[STATE : 2 * STATE, :] = low
    turned = jnp.transpose(wout)
    high, low = halves(turned)
    hf, lf = high.astype(f32), low.astype(f32)
    wb_ref[...] = jnp.concatenate([hf, lf, hf], axis=1).astype(bf16)


def prepare_call(nb, pc, cp, *arrays):
    length = nb * cp
    shapes = [
        ((2 * STATE, length), f32),
        ((8, length), f32),
        ((8, WAVE_INNER * HALF), jnp.int32),
        ((3 * LANES, 2 * LANES), bf16),
        ((2 * WAVE_INNER, LANES), f32),
        ((FIELDS, LANES), f32),
        ((UNITS, 6 * STATE + 16), bf16),
        ((2 * STATE, UNITS), bf16),
        ((4 * STATE, UNITS), bf16),
        ((UNITS, 3 * STATE), bf16),
    ]
    return pl.pallas_call(
        functools.partial(prepare_kernel, nb, pc, cp),
        out_shape=[jax.ShapeDtypeStruct(*s) for s in shapes],
        compiler_params=pltpu.CompilerParams(vmem_limit_bytes=VMEM_LIMIT),
        name="prepare",
    )(*arrays)


def advance_kernel(nb, cp, ndev, lc, owner_ref, arrived_ref, inverse_ref, dft_ref, turn_ref, amps_ref, cells_ref,
                   place_ref, wx_ref, wo_ref, wt_ref, wb_ref, out_ref, copies_ref,
                   grid_ref, pattern_ref, param_ref, force_ref, state_ref, slope_ref, adj_ref, grad_ref):
    length = nb * cp
    lane = iota((1, LANES), 1)
    rows = iota((FIELDS, LANES), 1)
    low_half = rows < HALF
    blocks = []
    for q in range(WAVE_INNER // 2):
        natural = lane + q * LANES
        wave = (natural % HALF) * WAVE_INNER + natural // HALF
        at = inverse_ref[0:1, pl.ds(q * LANES, LANES)]
        x = pick((nb, lambda i: arrived_ref[i]), at // LANES, at % LANES, 2 * FIELDS)
        x = jnp.where(wave < WAVES, x * jnp.where(wave == 0, 1.0, 2.0), 0.0)
        real, imag = x[:FIELDS], x[FIELDS:]
        blocks.append(jnp.where(low_half, real, pltpu.roll(imag, HALF, 1)))
        blocks.append(jnp.where(low_half, pltpu.roll(real, HALF, 1), imag))
    coeffs = jnp.concatenate(blocks, axis=0)
    high, low = halves(coeffs)
    partial = dot(high, dft_ref[0:LANES]) + dot(low, dft_ref[0:LANES]) + dot(high, dft_ref[2 * LANES : 3 * LANES])
    reals, imags = [], []
    for b in range(WAVE_INNER):
        y_real = partial[b * FIELDS : (b + 1) * FIELDS, :LANES]
        y_imag = partial[b * FIELDS : (b + 1) * FIELDS, LANES:]
        cosine, sine = turn_ref[b : b + 1, :], turn_ref[WAVE_INNER + b : WAVE_INNER + b + 1, :]
        reals.append(y_real * cosine - y_imag * sine)
        imags.append(y_real * sine + y_imag * cosine)
    half = WAVE_INNER // 2
    sums = [reals[b] + reals[WAVE_INNER - b] for b in range(1, half)]
    gaps = [imags[b] - imags[WAVE_INNER - b] for b in range(1, half)]
    for c in range(half + 1):
        even = reals[0] + reals[half] if c % 2 == 0 else reals[0] - reals[half]
        odd = None
        for b in range(1, half):
            turn = 2.0 * math.pi * (b * c % WAVE_INNER) / WAVE_INNER
            even = even + math.cos(turn) * sums[b - 1]
            term = math.sin(turn) * gaps[b - 1]
            odd = term if odd is None else odd + term
        grid_ref[c] = even - odd
        if 0 < c < half:
            grid_ref[WAVE_INNER - c] = even + odd
    amps = amps_ref[...]
    for q in range(length // LANES):
        at = pl.ds(q * LANES, LANES)
        column = place_ref[STEPS : STEPS + 1, at].astype(jnp.int32)
        found = pick((LON_OUTER, lambda i: grid_ref[i]), column // LANES, column % LANES, FIELDS)
        pattern_ref[:, at] = found
        high, low = halves(amps * found)
        param_ref[0:FIELDS, at] = high
        param_ref[FIELDS : 2 * FIELDS, at] = high
        param_ref[2 * FIELDS : 3 * FIELDS, at] = low
        row16 = iota((16, LANES), 0)
        for t in range(STEPS):
            force = place_ref[t : t + 1, at]
            force_high = force.astype(bf16).astype(f32)
            packed = jnp.where(row16 < 2, force_high, jnp.where(row16 == 2, force - force_high, 0.0))
            force_ref[t, :, at] = packed.astype(bf16)
    state_ref[...] = cells_ref[0:STATE, :]
    spans = [pl.ds(i * lc, lc) for i in range(length // lc)]
    wx, wo, wt, wb = wx_ref[...], wo_ref[...], wt_ref[...], wb_ref[...]
    for t in range(STEPS):
        for at in spans:
            state = state_ref[:, at]
            high, low = halves(state)
            joined = jnp.concatenate([high, high, low, param_ref[:, at], force_ref[t, :, at]], axis=0)
            hidden = jnp.tanh(dot(wx, joined))
            slope_ref[t, :, at] = 1.0 - hidden * hidden
            high, low = halves(hidden)
            moved = dot(wo, high)
            moved = moved[:STATE] + moved[STATE:] + dot(wo[:STATE], low)
            state_ref[:, at] = state + TIME_STEP * moved
    for t in reversed(range(STEPS)):
        for at in spans:
            if t == STEPS - 1:
                adjoint = state_ref[:, at] - cells_ref[STATE : 2 * STATE, at]
            else:
                adjoint = adj_ref[:, at]
            high, low = halves(TIME_STEP * adjoint)
            through = dot(wb, jnp.concatenate([high, high, low], axis=0)) * slope_ref[t, :, at]
            high, low = halves(through)
            both = dot(wt, high)
            both = both[: 2 * STATE] + both[2 * STATE :] + dot(wt[: 2 * STATE], low)
            adj_ref[:, at] = adjoint + both[:STATE]
            gained = both[STATE:]
            grad_ref[:, at] = gained if t == STEPS - 1 else grad_ref[:, at] + gained
    first_owner = owner_ref[0, 0]
    total = jnp.zeros((FIELDS, cp), f32)
    place = iota((FIELDS, cp), 1).astype(f32)
    for m in range(nb):
        owner = (first_owner + m) % nb
        at = pl.ds(m * cp, cp)
        grad = grad_ref[:, at]
        out_ref[owner, 0:STATE, :] = state_ref[:, at]
        out_ref[owner, STATE : 2 * STATE, :] = grad
        count = arrived_ref[owner, 0:1, COUNT_LANE : COUNT_LANE + 1]
        total = total + jnp.where(place < count, grad * pattern_ref[:, at], 0.0)
    summed = jnp.sum(total, axis=1, keepdims=True)
    diagonal = iota((FIELDS, FIELDS), 0) == iota((FIELDS, FIELDS), 1)
    along = jnp.sum(jnp.where(diagonal, summed, 0.0), axis=0, keepdims=True)
    copies_ref[...] = jnp.broadcast_to(along, (ndev, FIELDS))


def advance_call(nb, cp, ndev, owner_map, arrived, prepared):
    cells, place, inverse, dft, turn, amps, wx, wo, wt, wb = prepared
    length = nb * cp
    lc = 512
    vmem = pl.BlockSpec(memory_space=pltpu.VMEM)
    return pl.pallas_call(
        functools.partial(advance_kernel, nb, cp, ndev, lc),
        in_specs=[pl.BlockSpec(memory_space=pltpu.SMEM)] + [vmem] * 11,
        out_shape=[
            jax.ShapeDtypeStruct((nb, 2 * STATE, cp), f32),
            jax.ShapeDtypeStruct((ndev, FIELDS), f32),
        ],
        scratch_shapes=[
            pltpu.VMEM((LON_OUTER, FIELDS, LANES), f32),
            pltpu.VMEM((FIELDS, length), f32),
            pltpu.VMEM((3 * FIELDS, length), bf16),
            pltpu.VMEM((STEPS, 16, length), bf16),
            pltpu.VMEM((STATE, length), f32),
            pltpu.VMEM((STEPS, UNITS, length), f32),
            pltpu.VMEM((STATE, length), f32),
            pltpu.VMEM((FIELDS, length), f32),
        ],
        compiler_params=pltpu.CompilerParams(vmem_limit_bytes=VMEM_LIMIT),
        name="advance",
    )(owner_map[:, :LANES], arrived, inverse, dft, turn, amps, cells, place, wx, wo, wt, wb)


def owned_kernel(nb, cap, cp, scale, slot_ref, received_ref, parts_ref, final_ref, grad_ref, amp_ref):
    per_row = cp // LANES
    for q in range(slot_ref.shape[1] // LANES):
        at = pl.ds(q * LANES, LANES)
        slot = slot_ref[:, at]
        row = ((slot.astype(f32) + 0.5) * (1.0 / cap)).astype(jnp.int32)
        place = slot - row * cap
        piece = row * per_row + place // LANES

        def load(i):
            return received_ref[i // per_row, :, pl.ds(i % per_row * LANES, LANES)]

        found = pick((nb * per_row, load), piece, place % LANES, 2 * STATE)
        final_ref[:, at] = found[:STATE]
        grad_ref[:, at] = found[STATE:]
    amp_ref[...] = jnp.sum(parts_ref[...], axis=0, keepdims=True) * scale


def owned_call(nb, cap, cp, scale, owner_slot, received, parts):
    mean = owner_slot.shape[1]
    return pl.pallas_call(
        functools.partial(owned_kernel, nb, cap, cp, scale),
        out_shape=[
            jax.ShapeDtypeStruct((STATE, mean), f32),
            jax.ShapeDtypeStruct((FIELDS, mean), f32),
            jax.ShapeDtypeStruct((1, FIELDS), f32),
        ],
        compiler_params=pltpu.CompilerParams(vmem_limit_bytes=VMEM_LIMIT),
        name="owned",
    )(owner_slot, received, parts)


def body(
    spectra,
    pair_slot,
    land_column,
    owner_map,
    owner_slot,
    state_start,
    targets,
    amplitudes,
    weight_in,
    weight_out,
):
    nb = lax.axis_size("fld")
    ndev = lax.axis_size("band") * nb
    pc = spectra.shape[0]
    cap = ROW_MAX // nb
    cp = -(-cap // LANES) * LANES
    coeffs = fourier_call(nb, pc, cap, pair_slot, owner_slot, spectra)
    arrived = lax.all_to_all(coeffs, "fld", split_axis=0, concat_axis=0, tiled=True)
    prepared = prepare_call(
        nb, pc, cp, jnp.broadcast_to(pair_slot[:, None], (PAIRS, LANES)), land_column, state_start, targets,
        amplitudes[None, :], weight_in, weight_out,
    )
    outbound, copies = advance_call(nb, cp, ndev, owner_map, arrived, prepared)
    received = lax.all_to_all(outbound, "fld", split_axis=0, concat_axis=0, tiled=True)
    parts = lax.all_to_all(copies, ("band", "fld"), split_axis=0, concat_axis=0, tiled=True)
    scale = 1.0 / math.sqrt(ndev * ROW_MEAN)
    final_state, param_grad, amplitude_grad = owned_call(nb, cap, cp, scale, owner_slot, received, parts)
    return (final_state, param_grad, amplitude_grad[0])


def solution(mesh):
    return jax.shard_map(
        body,
        mesh=mesh,
        in_specs=(
            P("fld", None, None),
            P(),
            P(("band", "fld"), None),
            P(("band", "fld"), None),
            P(("band", "fld"), None),
            P(None, ("band", "fld"), None),
            P(None, ("band", "fld"), None),
            P(),
            P(),
            P(),
        ),
        out_specs=(P(None, ("band", "fld")), P(None, ("band", "fld")), P()),
        check_vma=False,
    )
```

```python
import functools
import math

import jax
import jax.numpy as jnp
from jax import lax
from jax.experimental import pallas as pl
from jax.experimental.pallas import tpu as pltpu
from jax.sharding import PartitionSpec as P

FIELDS = 16
STATE = 16
UNITS = 256
WAVES = 960
LONS = 2048
LATS = 1024
STEPS = 4
ROW_MEAN = 640
COEFS = 961
ROW_MAX = 1920
PAIRS = 480
TIME_STEP = 0.25

LANES = 128
HALF = LANES // 2
COUNT_LANE = HALF - 1
COEF_PAD = 1024
COEF_TILES = COEF_PAD // LANES
LAST = COEFS - (COEF_TILES - 1) * LANES
EARLY = (WAVES - PAIRS + 1) // LANES
LON_OUTER = LONS // LANES
WAVE_INNER = 16
VMEM_LIMIT = 60 * 1024 * 1024

f32 = jnp.float32
bf16 = jnp.bfloat16


def iota(shape, dim):
    return lax.broadcasted_iota(jnp.int32, shape, dim)


def sincos_turns(turns):
    part = turns - jnp.round(turns)
    quarter = jnp.round(4.0 * part)
    x = (part - 0.25 * quarter) * (2.0 * math.pi)
    y = x * x
    sine = x * (1.0 + y * (-1.0 / 6 + y * (1.0 / 120 + y * (-1.0 / 5040 + y * (1.0 / 362880)))))
    cosine = 1.0 + y * (-0.5 + y * (1.0 / 24 + y * (-1.0 / 720 + y * (1.0 / 40320))))
    swap = jnp.abs(quarter) == 1.0
    low_sine = jnp.where(swap, cosine, sine)
    low_cosine = jnp.where(swap, sine, cosine)
    sine_flip = (quarter == -1.0) | (jnp.abs(quarter) == 2.0)
    cosine_flip = (quarter == 1.0) | (jnp.abs(quarter) == 2.0)
    return jnp.where(sine_flip, -low_sine, low_sine), jnp.where(cosine_flip, -low_cosine, low_cosine)


def halves(x):
    high = x.astype(bf16)
    return high, (x - high.astype(f32)).astype(bf16)


def dot(a, b):
    return jnp.dot(a, b, preferred_element_type=f32)


def dot_last(a, b):
    return lax.dot_general(a, b, (((1,), (1,)), ((), ())), preferred_element_type=f32)


def pick(pieces, piece_at, lane_at, rows):
    count, load = pieces
    lane_full = jnp.broadcast_to(lane_at, (rows, LANES))
    total = None
    for i in range(count):
        got = jnp.take_along_axis(load(i), lane_full, axis=1)
        total = got if total is None else jnp.where(piece_at == i, got, total)
    return total


def fourier_kernel(nb, pc, cap, gc, pairs_ref, slot_ref, spec_ref, out_ref, buf, tab, thr, lhs, tail, sem):
    lane = iota((nb, LANES), 1)
    rows = pc * gc
    groups = 2 * FIELDS // gc
    copies = []
    for k in range(groups):
        at = pl.ds(k * gc, gc)
        copies.append(pltpu.make_async_copy(spec_ref.at[:, at, :], buf.at[:, at, :], sem.at[k]))
        copies[k].start()
    band = lax.axis_index("band")
    first = lax.axis_index("fld") * pc
    odd = (2 * (band * nb + iota((nb, LANES), 0)) + 1).astype(f32) * (1.0 / (4 * LATS))
    for t in range(COEF_TILES):
        column = lane + t * LANES
        if t == COEF_TILES - 1:
            column = jnp.where(lane < LAST, column, lane + EARLY * LANES)
        sine, cosine = sincos_turns(column.astype(f32) * odd)
        high, low = halves(jnp.concatenate([cosine, sine], axis=0))
        at = pl.ds(t * LANES, LANES)
        tab[0 : 2 * nb, at] = high
        tab[2 * nb : 4 * nb, at] = low
    row = jnp.zeros((nb, LANES), f32)
    for s in range(pc):
        pair = pairs_ref[first + s]
        row = jnp.where(lane % HALF == s, pair.astype(f32), row)
        thr[s * gc : (s + 1) * gc, :] = jnp.full((gc, LANES), WAVES - pair, jnp.int32)
    sine, cosine = sincos_turns(row * odd)
    is_odd = row - 2.0 * jnp.floor(row * 0.5) == 1.0
    alpha = jnp.where(is_odd, sine, cosine)
    beta = jnp.where(is_odd, cosine, -sine)
    sine, cosine = sincos_turns(odd)
    gamma = jnp.where(is_odd, cosine, -sine)
    delta = jnp.where(is_odd, sine, cosine)
    pieces = -(-rows // LANES)
    wide = iota((rows, LANES), 1)
    for k in range(groups):
        copies[k].wait()
        base = k * rows
        here = slice(base, base + rows)
        early = None
        for t in range(COEF_TILES):
            at = pl.ds(t * LANES, LANES)
            if t < COEF_TILES - 1:
                x = buf[:, k * gc : (k + 1) * gc, at].reshape(rows, LANES)
            else:
                x = buf[:, k * gc : (k + 1) * gc, t * LANES : COEFS].reshape(rows, LAST)
                x = jnp.concatenate([x, jnp.zeros((rows, LANES - LAST), f32)], axis=1)
            high = x.astype(bf16)
            whole = high.astype(f32)
            rest = x - whole
            lhs[0, here, at] = high
            lhs[1, here, at] = rest.astype(bf16)
            if t == EARLY:
                early = whole, rest
            if t > EARLY:
                column = wide + t * LANES
                if t == COEF_TILES - 1:
                    column = jnp.where(wide < LAST, column, wide + EARLY * LANES)
                    whole = jnp.where(wide < LAST, whole, early[0])
                    rest = jnp.where(wide < LAST, rest, early[1])
                second = column >= thr[...]
                at = pl.ds((t - EARLY - 1) * LANES, LANES)
                tail[0, here, at] = jnp.where(second, whole, 0.0).astype(bf16)
                tail[1, here, at] = jnp.where(second, rest, 0.0).astype(bf16)
        end = slice((EARLY + 1) * LANES, COEF_PAD)
        everything = contract(lhs[0, here, :], tab[...]) + contract(lhs[1, here, :], tab[...])
        shifted = contract(tail[0, here, :], tab[:, end]) + contract(tail[1, here, :], tab[:, end])
        everything = everything[: 2 * nb] + everything[2 * nb :]
        shifted = shifted[: 2 * nb] + shifted[2 * nb :]
        pad = [(0, 0), (0, pieces * LANES - rows)]
        first_part, shifted = jnp.pad(everything - shifted, pad), jnp.pad(shifted, pad)
        for g in range(gc):
            source = (iota((1, LANES), 1) % HALF) * gc + g
            piece_at, lane_at = source // LANES, source % LANES

            def gather(values):
                return pick((pieces, lambda i: values[:, i * LANES : (i + 1) * LANES]), piece_at, lane_at, nb)

            wave0 = alpha * gather(first_part[:nb]) + beta * gather(first_part[nb:])
            wave1 = gamma * gather(shifted[:nb]) + delta * gather(shifted[nb:])
            value = jnp.where(lane < HALF, wave0, wave1)
            value = jnp.where(lane % HALF < pc, value, 0.0)
            if k == 0 and g == 0:
                slot = jnp.broadcast_to(slot_ref[...], (nb, slot_ref.shape[1]))
                below = iota((nb, slot_ref.shape[1]), 0) * cap
                inside = (slot >= below) & (slot < below + cap)
                count = jnp.sum(jnp.where(inside, 1.0, 0.0), axis=1, keepdims=True)
                value = jnp.where(lane == COUNT_LANE, count, value)
            out_ref[:, k * gc + g, :] = value


def contract(values, table):
    return jnp.transpose(dot_last(values, table))


def fourier_call(nb, pc, cap, pair_slot, owner_slot, spectra):
    gc = 8
    rows = 2 * FIELDS * pc
    return pl.pallas_call(
        functools.partial(fourier_kernel, nb, pc, cap, gc),
        in_specs=[
            pl.BlockSpec(memory_space=pltpu.SMEM),
            pl.BlockSpec(memory_space=pltpu.VMEM),
            pl.BlockSpec(memory_space=pl.ANY),
        ],
        out_shape=jax.ShapeDtypeStruct((nb, 2 * FIELDS, LANES), f32),
        scratch_shapes=[
            pltpu.VMEM(spectra.shape, f32),
            pltpu.VMEM((4 * nb, COEF_PAD), bf16),
            pltpu.VMEM((pc * gc, LANES), jnp.int32),
            pltpu.VMEM((2, rows, COEF_PAD), bf16),
            pltpu.VMEM((2, rows, COEF_PAD - (EARLY + 1) * LANES), bf16),
            pltpu.SemaphoreType.DMA((2 * FIELDS // gc,)),
        ],
        compiler_params=pltpu.CompilerParams(vmem_limit_bytes=VMEM_LIMIT),
        name="fourier",
    )(pair_slot, owner_slot, spectra)


def prepare_kernel(nb, pc, cp, pairs_ref, land_ref, state_ref, target_ref, amp_ref, win_ref, wout_ref,
                   cells_ref, place_ref, inverse_ref, dft_ref, turn_ref, amps_ref,
                   wx_ref, wo_ref, wt_ref, wb_ref):
    lane = iota((1, LANES), 1)
    source_pieces = ROW_MAX // LANES
    row = lax.axis_index("band") * nb + lax.axis_index("fld")
    odd = (2 * row + 1).astype(f32) * (0.5 / (2 * LATS))
    sin_colat = sincos_turns(jnp.full((8, LANES), 1.0, f32) * odd)[0]
    joined = 2 * STATE
    for m in range(nb):
        for q in range(cp // LANES):
            source = nb * (q * LANES + lane) + m
            first = nb * q
            count = min(nb, source_pieces - first)
            at = pl.ds(m * cp + q * LANES, LANES)
            piece_at, lane_at = source // LANES - first, source % LANES

            def load(ref, i):
                return ref[:, 0, pl.ds((first + i) * LANES, LANES)]

            for k, ref in enumerate((state_ref, target_ref)):
                cells_ref[k * STATE : (k + 1) * STATE, at] = pick(
                    (count, functools.partial(load, ref)), piece_at, lane_at, STATE
                )

            def load_land(i):
                return jnp.broadcast_to(land_ref[:, pl.ds((first + i) * LANES, LANES)], (8, LANES))

            column = pick((count, load_land), piece_at, lane_at, 8)
            hour = iota((8, LANES), 0).astype(f32)
            turns = column.astype(f32) * (1.0 / LONS) + hour * (1.0 / 24.0)
            forcing = jnp.maximum(sincos_turns(turns)[1], 0.0) * sin_colat
            place_ref[:, at] = jnp.where(iota((8, LANES), 0) < STEPS, forcing, column.astype(f32))
    for q in range(WAVE_INNER // 2):
        natural = lane + q * LANES
        wave = (natural % HALF) * WAVE_INNER + natural // HALF
        pair = jnp.minimum(wave, WAVES - 1 - wave)
        total = jnp.zeros((8, LANES), jnp.int32)
        rows = iota((8, LANES), 0)
        for i in range(PAIRS // 8):
            here = i * 8 + rows
            arrives = here + ((here.astype(f32) + 0.5) * (1.0 / pc)).astype(jnp.int32) * (LANES - pc)
            total = total + jnp.where(pairs_ref[i * 8 : i * 8 + 8, :] == pair, arrives, 0)
        found = jnp.sum(total.astype(f32), axis=0, keepdims=True).astype(jnp.int32)
        inverse_ref[:, pl.ds(q * LANES, LANES)] = jnp.broadcast_to(
            found + jnp.where(wave >= PAIRS, HALF, 0), (8, LANES)
        )
    a = iota((HALF, LANES), 0)
    sine, cosine = sincos_turns((a * iota((HALF, LANES), 1)).astype(f32) * (1.0 / LANES))
    table = jnp.concatenate(
        [jnp.concatenate([cosine, sine], axis=1), jnp.concatenate([-sine, cosine], axis=1)], axis=0
    )
    high, low = halves(table)
    dft_ref[0:LANES, :] = high
    dft_ref[LANES : 2 * LANES, :] = high
    dft_ref[2 * LANES : 3 * LANES, :] = low
    b = iota((WAVE_INNER, LANES), 0)
    sine, cosine = sincos_turns((b * iota((WAVE_INNER, LANES), 1)).astype(f32) * (1.0 / LONS))
    turn_ref[0:WAVE_INNER, :] = cosine
    turn_ref[WAVE_INNER : 2 * WAVE_INNER, :] = sine
    amp = jnp.broadcast_to(amp_ref[...], (FIELDS, FIELDS))
    diagonal = iota((FIELDS, FIELDS), 0) == iota((FIELDS, FIELDS), 1)
    amps_ref[...] = jnp.broadcast_to(
        jnp.sum(jnp.where(diagonal, amp, 0.0), axis=1, keepdims=True), (FIELDS, LANES)
    )
    win = win_ref[...]
    wout = wout_ref[...]
    high, low = halves(win)
    s, p = slice(0, STATE), slice(STATE, joined)
    tail = jnp.where(iota((UNITS, STATE), 1) == 0, high[:, joined:].astype(f32), 0.0)
    tail = jnp.where(iota((UNITS, STATE), 1) == 1, low[:, joined:].astype(f32), tail)
    tail = jnp.where(iota((UNITS, STATE), 1) == 2, high[:, joined:].astype(f32), tail)
    hf, lf = high.astype(f32), low.astype(f32)
    wx_ref[...] = jnp.concatenate(
        [hf[:, s], lf[:, s], hf[:, s], hf[:, p], lf[:, p], hf[:, p], tail], axis=1
    ).astype(bf16)
    turned = jnp.transpose(win)[:joined]
    high, low = halves(turned)
    wt_ref[0:joined, :] = high
    wt_ref[joined : 2 * joined, :] = low
    high, low = halves(wout)
    wo_ref[0:STATE, :] = high
    wo_ref[STATE : 2 * STATE, :] = low
    turned = jnp.transpose(wout)
    high, low = halves(turned)
    hf, lf = high.astype(f32), low.astype(f32)
    wb_ref[...] = jnp.concatenate([hf, lf, hf], axis=1).astype(bf16)


def prepare_call(nb, pc, cp, *arrays):
    length = nb * cp
    shapes = [
        ((2 * STATE, length), f32),
        ((8, length), f32),
        ((8, WAVE_INNER * HALF), jnp.int32),
        ((3 * LANES, 2 * LANES), bf16),
        ((2 * WAVE_INNER, LANES), f32),
        ((FIELDS, LANES), f32),
        ((UNITS, 6 * STATE + 16), bf16),
        ((2 * STATE, UNITS), bf16),
        ((4 * STATE, UNITS), bf16),
        ((UNITS, 3 * STATE), bf16),
    ]
    return pl.pallas_call(
        functools.partial(prepare_kernel, nb, pc, cp),
        out_shape=[jax.ShapeDtypeStruct(*s) for s in shapes],
        compiler_params=pltpu.CompilerParams(vmem_limit_bytes=VMEM_LIMIT),
        name="prepare",
    )(*arrays)


def advance_kernel(nb, cp, ndev, lc, owner_ref, arrived_ref, inverse_ref, dft_ref, turn_ref, amps_ref, cells_ref,
                   place_ref, wx_ref, wo_ref, wt_ref, wb_ref, out_ref, copies_ref,
                   grid_ref, pattern_ref, param_ref, force_ref, state_ref, slope_ref, adj_ref, grad_ref):
    length = nb * cp
    lane = iota((1, LANES), 1)
    rows = iota((FIELDS, LANES), 1)
    low_half = rows < HALF
    blocks = []
    for q in range(WAVE_INNER // 2):
        natural = lane + q * LANES
        wave = (natural % HALF) * WAVE_INNER + natural // HALF
        at = inverse_ref[0:1, pl.ds(q * LANES, LANES)]
        x = pick((nb, lambda i: arrived_ref[i]), at // LANES, at % LANES, 2 * FIELDS)
        x = jnp.where(wave < WAVES, x * jnp.where(wave == 0, 1.0, 2.0), 0.0)
        real, imag = x[:FIELDS], x[FIELDS:]
        blocks.append(jnp.where(low_half, real, pltpu.roll(imag, HALF, 1)))
        blocks.append(jnp.where(low_half, pltpu.roll(real, HALF, 1), imag))
    coeffs = jnp.concatenate(blocks, axis=0)
    high, low = halves(coeffs)
    partial = dot(high, dft_ref[0:LANES]) + dot(low, dft_ref[0:LANES]) + dot(high, dft_ref[2 * LANES : 3 * LANES])
    reals, imags = [], []
    for b in range(WAVE_INNER):
        y_real = partial[b * FIELDS : (b + 1) * FIELDS, :LANES]
        y_imag = partial[b * FIELDS : (b + 1) * FIELDS, LANES:]
        cosine, sine = turn_ref[b : b + 1, :], turn_ref[WAVE_INNER + b : WAVE_INNER + b + 1, :]
        reals.append(y_real * cosine - y_imag * sine)
        imags.append(y_real * sine + y_imag * cosine)
    half = WAVE_INNER // 2
    sums = [reals[b] + reals[WAVE_INNER - b] for b in range(1, half)]
    gaps = [imags[b] - imags[WAVE_INNER - b] for b in range(1, half)]
    for c in range(half + 1):
        even = reals[0] + reals[half] if c % 2 == 0 else reals[0] - reals[half]
        odd = None
        for b in range(1, half):
            turn = 2.0 * math.pi * (b * c % WAVE_INNER) / WAVE_INNER
            even = even + math.cos(turn) * sums[b - 1]
            term = math.sin(turn) * gaps[b - 1]
            odd = term if odd is None else odd + term
        grid_ref[c] = even - odd
        if 0 < c < half:
            grid_ref[WAVE_INNER - c] = even + odd
    amps = amps_ref[...]
    for q in range(length // LANES):
        at = pl.ds(q * LANES, LANES)
        column = place_ref[STEPS : STEPS + 1, at].astype(jnp.int32)
        found = pick((LON_OUTER, lambda i: grid_ref[i]), column // LANES, column % LANES, FIELDS)
        pattern_ref[:, at] = found
        high, low = halves(amps * found)
        param_ref[0:FIELDS, at] = high
        param_ref[FIELDS : 2 * FIELDS, at] = high
        param_ref[2 * FIELDS : 3 * FIELDS, at] = low
        row16 = iota((16, LANES), 0)
        for t in range(STEPS):
            force = place_ref[t : t + 1, at]
            force_high = force.astype(bf16).astype(f32)
            packed = jnp.where(row16 < 2, force_high, jnp.where(row16 == 2, force - force_high, 0.0))
            force_ref[t, :, at] = packed.astype(bf16)
    state_ref[...] = cells_ref[0:STATE, :]
    spans = [pl.ds(i * lc, lc) for i in range(length // lc)]
    wx, wo, wt, wb = wx_ref[...], wo_ref[...], wt_ref[...], wb_ref[...]
    for t in range(STEPS):
        for at in spans:
            state = state_ref[:, at]
            high, low = halves(state)
            joined = jnp.concatenate([high, high, low, param_ref[:, at], force_ref[t, :, at]], axis=0)
            hidden = jnp.tanh(dot(wx, joined))
            slope_ref[t, :, at] = 1.0 - hidden * hidden
            high, low = halves(hidden)
            moved = dot(wo, high)
            moved = moved[:STATE] + moved[STATE:] + dot(wo[:STATE], low)
            state_ref[:, at] = state + TIME_STEP * moved
    for t in reversed(range(STEPS)):
        for at in spans:
            if t == STEPS - 1:
                adjoint = state_ref[:, at] - cells_ref[STATE : 2 * STATE, at]
            else:
                adjoint = adj_ref[:, at]
            high, low = halves(TIME_STEP * adjoint)
            through = dot(wb, jnp.concatenate([high, high, low], axis=0)) * slope_ref[t, :, at]
            high, low = halves(through)
            both = dot(wt, high)
            both = both[: 2 * STATE] + both[2 * STATE :] + dot(wt[: 2 * STATE], low)
            adj_ref[:, at] = adjoint + both[:STATE]
            gained = both[STATE:]
            grad_ref[:, at] = gained if t == STEPS - 1 else grad_ref[:, at] + gained
    first_owner = owner_ref[0, 0]
    total = jnp.zeros((FIELDS, cp), f32)
    place = iota((FIELDS, cp), 1).astype(f32)
    for m in range(nb):
        owner = (first_owner + m) % nb
        at = pl.ds(m * cp, cp)
        grad = grad_ref[:, at]
        out_ref[owner, 0:STATE, :] = state_ref[:, at]
        out_ref[owner, STATE : 2 * STATE, :] = grad
        count = arrived_ref[owner, 0:1, COUNT_LANE : COUNT_LANE + 1]
        total = total + jnp.where(place < count, grad * pattern_ref[:, at], 0.0)
    summed = jnp.sum(total, axis=1, keepdims=True)
    diagonal = iota((FIELDS, FIELDS), 0) == iota((FIELDS, FIELDS), 1)
    along = jnp.sum(jnp.where(diagonal, summed, 0.0), axis=0, keepdims=True)
    copies_ref[...] = jnp.broadcast_to(along, (ndev, FIELDS))


def advance_call(nb, cp, ndev, owner_map, arrived, prepared):
    cells, place, inverse, dft, turn, amps, wx, wo, wt, wb = prepared
    length = nb * cp
    lc = 512
    vmem = pl.BlockSpec(memory_space=pltpu.VMEM)
    return pl.pallas_call(
        functools.partial(advance_kernel, nb, cp, ndev, lc),
        in_specs=[pl.BlockSpec(memory_space=pltpu.SMEM)] + [vmem] * 11,
        out_shape=[
            jax.ShapeDtypeStruct((nb, 2 * STATE, cp), f32),
            jax.ShapeDtypeStruct((ndev, FIELDS), f32),
        ],
        scratch_shapes=[
            pltpu.VMEM((LON_OUTER, FIELDS, LANES), f32),
            pltpu.VMEM((FIELDS, length), f32),
            pltpu.VMEM((3 * FIELDS, length), bf16),
            pltpu.VMEM((STEPS, 16, length), bf16),
            pltpu.VMEM((STATE, length), f32),
            pltpu.VMEM((STEPS, UNITS, length), f32),
            pltpu.VMEM((STATE, length), f32),
            pltpu.VMEM((FIELDS, length), f32),
        ],
        compiler_params=pltpu.CompilerParams(vmem_limit_bytes=VMEM_LIMIT),
        name="advance",
    )(owner_map[:, :LANES], arrived, inverse, dft, turn, amps, cells, place, wx, wo, wt, wb)


def owned_kernel(nb, cap, cp, scale, slot_ref, received_ref, parts_ref, final_ref, grad_ref, amp_ref):
    per_row = cp // LANES
    for q in range(slot_ref.shape[1] // LANES):
        at = pl.ds(q * LANES, LANES)
        slot = slot_ref[:, at]
        row = ((slot.astype(f32) + 0.5) * (1.0 / cap)).astype(jnp.int32)
        place = slot - row * cap
        piece = row * per_row + place // LANES

        def load(i):
            return received_ref[i // per_row, :, pl.ds(i % per_row * LANES, LANES)]

        found = pick((nb * per_row, load), piece, place % LANES, 2 * STATE)
        final_ref[:, at] = found[:STATE]
        grad_ref[:, at] = found[STATE:]
    amp_ref[...] = jnp.sum(parts_ref[...], axis=0, keepdims=True) * scale


def owned_call(nb, cap, cp, scale, owner_slot, received, parts):
    mean = owner_slot.shape[1]
    return pl.pallas_call(
        functools.partial(owned_kernel, nb, cap, cp, scale),
        out_shape=[
            jax.ShapeDtypeStruct((STATE, mean), f32),
            jax.ShapeDtypeStruct((FIELDS, mean), f32),
            jax.ShapeDtypeStruct((1, FIELDS), f32),
        ],
        compiler_params=pltpu.CompilerParams(vmem_limit_bytes=VMEM_LIMIT),
        name="owned",
    )(owner_slot, received, parts)


def body(
    spectra,
    pair_slot,
    land_column,
    owner_map,
    owner_slot,
    state_start,
    targets,
    amplitudes,
    weight_in,
    weight_out,
):
    nb = lax.axis_size("fld")
    ndev = lax.axis_size("band") * nb
    pc = spectra.shape[0]
    cap = ROW_MAX // nb
    cp = -(-cap // LANES) * LANES
    coeffs = fourier_call(nb, pc, cap, pair_slot, owner_slot, spectra)
    arrived = lax.all_to_all(coeffs, "fld", split_axis=0, concat_axis=0, tiled=True)
    prepared = prepare_call(
        nb, pc, cp, jnp.broadcast_to(pair_slot[:, None], (PAIRS, LANES)), land_column, state_start, targets,
        amplitudes[None, :], weight_in, weight_out,
    )
    outbound, copies = advance_call(nb, cp, ndev, owner_map, arrived, prepared)
    received = lax.all_to_all(outbound, "fld", split_axis=0, concat_axis=0, tiled=True)
    parts = lax.all_to_all(copies, ("band", "fld"), split_axis=0, concat_axis=0, tiled=True)
    scale = 1.0 / math.sqrt(ndev * ROW_MEAN)
    final_state, param_grad, amplitude_grad = owned_call(nb, cap, cp, scale, owner_slot, received, parts)
    return (final_state, param_grad, amplitude_grad[0])


def solution(mesh):
    return jax.shard_map(
        body,
        mesh=mesh,
        in_specs=(
            P("fld", None, None),
            P(),
            P(("band", "fld"), None),
            P(("band", "fld"), None),
            P(("band", "fld"), None),
            P(None, ("band", "fld"), None),
            P(None, ("band", "fld"), None),
            P(),
            P(),
            P(),
        ),
        out_specs=(P(None, ("band", "fld")), P(None, ("band", "fld")), P()),
        check_vma=False,
    )
```

```python
import functools
import math

import jax
import jax.numpy as jnp
from jax import lax
from jax.experimental import pallas as pl
from jax.experimental.pallas import tpu as pltpu
from jax.sharding import PartitionSpec as P

FIELDS = 16
STATE = 16
UNITS = 256
WAVES = 960
LONS = 2048
LATS = 1024
STEPS = 4
ROW_MEAN = 640
COEFS = 961
ROW_MAX = 1920
PAIRS = 480
TIME_STEP = 0.25

LANES = 128
HALF = LANES // 2
COUNT_LANE = HALF - 1
COEF_PAD = 1024
COEF_TILES = COEF_PAD // LANES
LAST = COEFS - (COEF_TILES - 1) * LANES
EARLY = (WAVES - PAIRS + 1) // LANES
LON_OUTER = LONS // LANES
WAVE_INNER = 16
VMEM_LIMIT = 60 * 1024 * 1024

f32 = jnp.float32
bf16 = jnp.bfloat16


def iota(shape, dim):
    return lax.broadcasted_iota(jnp.int32, shape, dim)


def sincos_turns(turns):
    part = turns - jnp.round(turns)
    quarter = jnp.round(4.0 * part)
    x = (part - 0.25 * quarter) * (2.0 * math.pi)
    y = x * x
    sine = x * (1.0 + y * (-1.0 / 6 + y * (1.0 / 120 + y * (-1.0 / 5040 + y * (1.0 / 362880)))))
    cosine = 1.0 + y * (-0.5 + y * (1.0 / 24 + y * (-1.0 / 720 + y * (1.0 / 40320))))
    swap = jnp.abs(quarter) == 1.0
    low_sine = jnp.where(swap, cosine, sine)
    low_cosine = jnp.where(swap, sine, cosine)
    sine_flip = (quarter == -1.0) | (jnp.abs(quarter) == 2.0)
    cosine_flip = (quarter == 1.0) | (jnp.abs(quarter) == 2.0)
    return jnp.where(sine_flip, -low_sine, low_sine), jnp.where(cosine_flip, -low_cosine, low_cosine)


def halves(x):
    high = x.astype(bf16)
    return high, (x - high.astype(f32)).astype(bf16)


def dot(a, b):
    return jnp.dot(a, b, preferred_element_type=f32)


def dot_last(a, b):
    return lax.dot_general(a, b, (((1,), (1,)), ((), ())), preferred_element_type=f32)


def pick(pieces, piece_at, lane_at, rows):
    count, load = pieces
    lane_full = jnp.broadcast_to(lane_at, (rows, LANES))
    total = None
    for i in range(count):
        got = jnp.take_along_axis(load(i), lane_full, axis=1)
        total = got if total is None else jnp.where(piece_at == i, got, total)
    return total


def fourier_kernel(nb, pc, cap, gc, pairs_ref, slot_ref, spec_ref, out_ref, buf, tab, thr, lhs, tail, sem):
    lane = iota((nb, LANES), 1)
    rows = pc * gc
    groups = 2 * FIELDS // gc
    copies = []
    for k in range(groups):
        at = pl.ds(k * gc, gc)
        copies.append(pltpu.make_async_copy(spec_ref.at[:, at, :], buf.at[:, at, :], sem.at[k]))
        copies[k].start()
    band = lax.axis_index("band")
    first = lax.axis_index("fld") * pc
    odd = (2 * (band * nb + iota((nb, LANES), 0)) + 1).astype(f32) * (1.0 / (4 * LATS))
    for t in range(COEF_TILES):
        column = lane + t * LANES
        if t == COEF_TILES - 1:
            column = jnp.where(lane < LAST, column, lane + EARLY * LANES)
        sine, cosine = sincos_turns(column.astype(f32) * odd)
        high, low = halves(jnp.concatenate([cosine, sine], axis=0))
        at = pl.ds(t * LANES, LANES)
        tab[0 : 2 * nb, at] = high
        tab[2 * nb : 4 * nb, at] = low
    pieces = -(-rows // LANES)
    per_piece = LANES // gc
    sine1, cosine1 = sincos_turns(odd)
    factors = []
    for i in range(pieces):
        row = jnp.zeros((nb, LANES), f32)
        for s in range(i * per_piece, min((i + 1) * per_piece, pc)):
            pair = pairs_ref[first + s]
            row = jnp.where(lane // gc == s - i * per_piece, pair.astype(f32), row)
            thr[s * gc : (s + 1) * gc, :] = jnp.full((gc, LANES), WAVES - pair, jnp.int32)
        sine, cosine = sincos_turns(row * odd)
        is_odd = row - 2.0 * jnp.floor(row * 0.5) == 1.0
        factors.append(
            (
                jnp.where(is_odd, sine, cosine),
                jnp.where(is_odd, cosine, -sine),
                jnp.where(is_odd, cosine1, -sine1),
                jnp.where(is_odd, sine1, cosine1),
            )
        )
    wide = iota((rows, LANES), 1)
    for k in range(groups):
        copies[k].wait()
        base = k * rows
        here = slice(base, base + rows)
        early = None
        for t in range(COEF_TILES):
            at = pl.ds(t * LANES, LANES)
            if t < COEF_TILES - 1:
                x = buf[:, k * gc : (k + 1) * gc, at].reshape(rows, LANES)
            else:
                x = buf[:, k * gc : (k + 1) * gc, t * LANES : COEFS].reshape(rows, LAST)
                x = jnp.concatenate([x, jnp.zeros((rows, LANES - LAST), f32)], axis=1)
            high = x.astype(bf16)
            whole = high.astype(f32)
            rest = x - whole
            lhs[0, here, at] = high
            lhs[1, here, at] = rest.astype(bf16)
            if t == EARLY:
                early = whole, rest
            if t > EARLY:
                column = wide + t * LANES
                if t == COEF_TILES - 1:
                    column = jnp.where(wide < LAST, column, wide + EARLY * LANES)
                    whole = jnp.where(wide < LAST, whole, early[0])
                    rest = jnp.where(wide < LAST, rest, early[1])
                second = column >= thr[...]
                at = pl.ds((t - EARLY - 1) * LANES, LANES)
                tail[0, here, at] = jnp.where(second, whole, 0.0).astype(bf16)
                tail[1, here, at] = jnp.where(second, rest, 0.0).astype(bf16)
        end = slice((EARLY + 1) * LANES, COEF_PAD)
        everything = contract(lhs[0, here, :], tab[...]) + contract(lhs[1, here, :], tab[...])
        shifted = contract(tail[0, here, :], tab[:, end]) + contract(tail[1, here, :], tab[:, end])
        everything = everything[: 2 * nb] + everything[2 * nb :]
        shifted = shifted[: 2 * nb] + shifted[2 * nb :]
        pad = [(0, 0), (0, pieces * LANES - rows)]
        first_part, shifted = jnp.pad(everything - shifted, pad), jnp.pad(shifted, pad)
        waves = []
        for i, (alpha, beta, gamma, delta) in enumerate(factors):
            at = slice(i * LANES, (i + 1) * LANES)
            waves.append(alpha * first_part[:nb, at] + beta * first_part[nb:, at])
            waves.append(gamma * shifted[:nb, at] + delta * shifted[nb:, at])
        for g in range(gc):
            source = (iota((1, LANES), 1) % HALF) * gc + g
            piece_at = 2 * (source // LANES) + iota((1, LANES), 1) // HALF
            value = pick((2 * pieces, lambda i: waves[i]), piece_at, source % LANES, nb)
            value = jnp.where(lane % HALF < pc, value, 0.0)
            if k == 0 and g == 0:
                slot = jnp.broadcast_to(slot_ref[...], (nb, slot_ref.shape[1]))
                below = iota((nb, slot_ref.shape[1]), 0) * cap
                inside = (slot >= below) & (slot < below + cap)
                count = jnp.sum(jnp.where(inside, 1.0, 0.0), axis=1, keepdims=True)
                value = jnp.where(lane == COUNT_LANE, count, value)
            out_ref[:, k * gc + g, :] = value


def contract(values, table):
    return jnp.transpose(dot_last(values, table))


def fourier_call(nb, pc, cap, pair_slot, owner_slot, spectra):
    gc = 8
    rows = 2 * FIELDS * pc
    return pl.pallas_call(
        functools.partial(fourier_kernel, nb, pc, cap, gc),
        in_specs=[
            pl.BlockSpec(memory_space=pltpu.SMEM),
            pl.BlockSpec(memory_space=pltpu.VMEM),
            pl.BlockSpec(memory_space=pl.ANY),
        ],
        out_shape=jax.ShapeDtypeStruct((nb, 2 * FIELDS, LANES), f32),
        scratch_shapes=[
            pltpu.VMEM(spectra.shape, f32),
            pltpu.VMEM((4 * nb, COEF_PAD), bf16),
            pltpu.VMEM((pc * gc, LANES), jnp.int32),
            pltpu.VMEM((2, rows, COEF_PAD), bf16),
            pltpu.VMEM((2, rows, COEF_PAD - (EARLY + 1) * LANES), bf16),
            pltpu.SemaphoreType.DMA((2 * FIELDS // gc,)),
        ],
        compiler_params=pltpu.CompilerParams(vmem_limit_bytes=VMEM_LIMIT),
        name="fourier",
    )(pair_slot, owner_slot, spectra)


def prepare_kernel(nb, pc, cp, pairs_ref, owner_ref, land_ref, state_ref, target_ref, amp_ref, win_ref, wout_ref,
                   cells_ref, place_ref, inverse_ref, dft_ref, turn_ref, amps_ref,
                   wx_ref, wo_ref, wt_ref, wb_ref):
    lane = iota((1, LANES), 1)
    source_pieces = ROW_MAX // LANES
    row = lax.axis_index("band") * nb + lax.axis_index("fld")
    odd = (2 * row + 1).astype(f32) * (0.5 / (2 * LATS))
    sin_colat = sincos_turns(jnp.full((8, LANES), 1.0, f32) * odd)[0]
    joined = 2 * STATE
    for m in range(nb):
        for q in range(cp // LANES):
            source = nb * (q * LANES + lane) + m
            first = nb * q
            count = min(nb, source_pieces - first)
            at = pl.ds(m * cp + q * LANES, LANES)
            piece_at, lane_at = source // LANES - first, source % LANES

            def load(ref, i):
                return ref[:, 0, pl.ds((first + i) * LANES, LANES)]

            for k, ref in enumerate((state_ref, target_ref)):
                cells_ref[k * STATE : (k + 1) * STATE, at] = pick(
                    (count, functools.partial(load, ref)), piece_at, lane_at, STATE
                )

            def load_land(i):
                return jnp.broadcast_to(land_ref[:, pl.ds((first + i) * LANES, LANES)], (8, LANES))

            column = pick((count, load_land), piece_at, lane_at, 8)
            hour = iota((8, LANES), 0).astype(f32)
            turns = column.astype(f32) * (1.0 / LONS) + hour * (1.0 / 24.0)
            forcing = jnp.maximum(sincos_turns(turns)[1], 0.0) * sin_colat
            rest = jnp.where(iota((8, LANES), 0) == STEPS, column, owner_ref[0:1, 0:1]).astype(f32)
            place_ref[:, at] = jnp.where(iota((8, LANES), 0) < STEPS, forcing, rest)
    natural = iota((8, LANES), 0) * LANES + iota((8, LANES), 1)
    wave = (natural % HALF) * WAVE_INNER + natural // HALF
    pair = jnp.minimum(wave, WAVES - 1 - wave)
    totals = [jnp.where(wave >= PAIRS, HALF, 0)] + [jnp.zeros((8, LANES), jnp.int32)] * 3
    for i in range(PAIRS):
        arrives = i // pc * LANES + i % pc
        totals[i % 4] = jnp.where(pair == pairs_ref[i], totals[i % 4] + arrives, totals[i % 4])
    inverse_ref[...] = totals[0] + totals[1] + totals[2] + totals[3]
    a = iota((HALF, LANES), 0)
    sine, cosine = sincos_turns((a * iota((HALF, LANES), 1)).astype(f32) * (1.0 / LANES))
    table = jnp.concatenate(
        [jnp.concatenate([cosine, sine], axis=1), jnp.concatenate([-sine, cosine], axis=1)], axis=0
    )
    high, low = halves(table)
    dft_ref[0:LANES, :] = high
    dft_ref[LANES : 2 * LANES, :] = high
    dft_ref[2 * LANES : 3 * LANES, :] = low
    b = iota((WAVE_INNER, LANES), 0)
    sine, cosine = sincos_turns((b * iota((WAVE_INNER, LANES), 1)).astype(f32) * (1.0 / LONS))
    turn_ref[0:WAVE_INNER, :] = cosine
    turn_ref[WAVE_INNER : 2 * WAVE_INNER, :] = sine
    amp = jnp.broadcast_to(amp_ref[...], (FIELDS, FIELDS))
    diagonal = iota((FIELDS, FIELDS), 0) == iota((FIELDS, FIELDS), 1)
    amps_ref[...] = jnp.broadcast_to(
        jnp.sum(jnp.where(diagonal, amp, 0.0), axis=1, keepdims=True), (FIELDS, LANES)
    )
    turned = win_ref[...]
    wout = wout_ref[...]
    high, low = halves(turned[:joined])
    wt_ref[0:joined, :] = high
    wt_ref[joined : 2 * joined, :] = low
    high, low = halves(jnp.transpose(turned))
    s, p = slice(0, STATE), slice(STATE, joined)
    tail = jnp.where(iota((UNITS, STATE), 1) == 0, high[:, joined:].astype(f32), 0.0)
    tail = jnp.where(iota((UNITS, STATE), 1) == 1, low[:, joined:].astype(f32), tail)
    tail = jnp.where(iota((UNITS, STATE), 1) == 2, high[:, joined:].astype(f32), tail)
    hf, lf = high.astype(f32), low.astype(f32)
    wx_ref[...] = jnp.concatenate(
        [hf[:, s], lf[:, s], hf[:, s], hf[:, p], lf[:, p], hf[:, p], tail], axis=1
    ).astype(bf16)
    high, low = halves(wout)
    wo_ref[0:STATE, :] = high
    wo_ref[STATE : 2 * STATE, :] = low
    turned = jnp.transpose(wout)
    high, low = halves(turned)
    hf, lf = high.astype(f32), low.astype(f32)
    wb_ref[...] = jnp.concatenate([hf, lf, hf], axis=1).astype(bf16)


def prepare_call(nb, pc, cp, *arrays):
    length = nb * cp
    shapes = [
        ((2 * STATE, length), f32),
        ((8, length), f32),
        ((8, LANES), jnp.int32),
        ((3 * LANES, 2 * LANES), bf16),
        ((2 * WAVE_INNER, LANES), f32),
        ((FIELDS, LANES), f32),
        ((UNITS, 6 * STATE + 16), bf16),
        ((2 * STATE, UNITS), bf16),
        ((4 * STATE, UNITS), bf16),
        ((UNITS, 3 * STATE), bf16),
    ]
    vmem = pl.BlockSpec(memory_space=pltpu.VMEM)
    return pl.pallas_call(
        functools.partial(prepare_kernel, nb, pc, cp),
        in_specs=[pl.BlockSpec(memory_space=pltpu.SMEM)] + [vmem] * (len(arrays) - 1),
        out_shape=[jax.ShapeDtypeStruct(*s) for s in shapes],
        compiler_params=pltpu.CompilerParams(vmem_limit_bytes=VMEM_LIMIT),
        name="prepare",
    )(*arrays)


def advance_kernel(nb, cap, cp, lc, arrived_ref, inverse_ref, dft_ref, turn_ref, amps_ref, cells_ref,
                   place_ref, wx_ref, wo_ref, wt_ref, wb_ref, out_ref,
                   grid_ref, pattern_ref, param_ref, force_ref, state_ref, slope_ref, adj_ref, grad_ref):
    length = nb * cp
    lane = iota((1, LANES), 1)
    rows = iota((FIELDS, LANES), 1)
    low_half = rows < HALF
    blocks = []
    for q in range(WAVE_INNER // 2):
        natural = lane + q * LANES
        wave = (natural % HALF) * WAVE_INNER + natural // HALF
        at = inverse_ref[q : q + 1, :]
        x = pick((nb, lambda i: arrived_ref[i]), at // LANES, at % LANES, 2 * FIELDS)
        x = jnp.where(wave < WAVES, x * jnp.where(wave == 0, 1.0, 2.0), 0.0)
        real, imag = x[:FIELDS], x[FIELDS:]
        blocks.append(jnp.where(low_half, real, pltpu.roll(imag, HALF, 1)))
        blocks.append(jnp.where(low_half, pltpu.roll(real, HALF, 1), imag))
    coeffs = jnp.concatenate(blocks, axis=0)
    high, low = halves(coeffs)
    partial = dot(high, dft_ref[0:LANES]) + dot(low, dft_ref[0:LANES]) + dot(high, dft_ref[2 * LANES : 3 * LANES])
    reals, imags = [], []
    for b in range(WAVE_INNER):
        y_real = partial[b * FIELDS : (b + 1) * FIELDS, :LANES]
        y_imag = partial[b * FIELDS : (b + 1) * FIELDS, LANES:]
        cosine, sine = turn_ref[b : b + 1, :], turn_ref[WAVE_INNER + b : WAVE_INNER + b + 1, :]
        reals.append(y_real * cosine - y_imag * sine)
        imags.append(y_real * sine + y_imag * cosine)
    half = WAVE_INNER // 2
    sums = [reals[b] + reals[WAVE_INNER - b] for b in range(1, half)]
    gaps = [imags[b] - imags[WAVE_INNER - b] for b in range(1, half)]
    for c in range(half + 1):
        even = reals[0] + reals[half] if c % 2 == 0 else reals[0] - reals[half]
        odd = None
        for b in range(1, half):
            turn = 2.0 * math.pi * (b * c % WAVE_INNER) / WAVE_INNER
            even = even + math.cos(turn) * sums[b - 1]
            term = math.sin(turn) * gaps[b - 1]
            odd = term if odd is None else odd + term
        grid_ref[c] = even - odd
        if 0 < c < half:
            grid_ref[WAVE_INNER - c] = even + odd
    amps = amps_ref[...]
    for q in range(length // LANES):
        at = pl.ds(q * LANES, LANES)
        column = place_ref[STEPS : STEPS + 1, at].astype(jnp.int32)
        found = pick((LON_OUTER, lambda i: grid_ref[i]), column // LANES, column % LANES, FIELDS)
        pattern_ref[:, at] = found
        high, low = halves(amps * found)
        param_ref[0:FIELDS, at] = high
        param_ref[FIELDS : 2 * FIELDS, at] = high
        param_ref[2 * FIELDS : 3 * FIELDS, at] = low
        row16 = iota((16, LANES), 0)
        for t in range(STEPS):
            force = place_ref[t : t + 1, at]
            force_high = force.astype(bf16).astype(f32)
            packed = jnp.where(row16 < 2, force_high, jnp.where(row16 == 2, force - force_high, 0.0))
            force_ref[t, :, at] = packed.astype(bf16)
    state_ref[...] = cells_ref[0:STATE, :]
    spans = [pl.ds(i * lc, lc) for i in range(length // lc)]
    wx, wo, wt, wb = wx_ref[...], wo_ref[...], wt_ref[...], wb_ref[...]
    for t in range(STEPS):
        for at in spans:
            state = state_ref[:, at]
            high, low = halves(state)
            joined = jnp.concatenate([high, high, low, param_ref[:, at], force_ref[t, :, at]], axis=0)
            hidden = jnp.tanh(dot(wx, joined))
            slope_ref[t, :, at] = 1.0 - hidden * hidden
            high, low = halves(hidden)
            moved = dot(wo, high)
            moved = moved[:STATE] + moved[STATE:] + dot(wo[:STATE], low)
            state_ref[:, at] = state + TIME_STEP * moved
    for t in reversed(range(STEPS)):
        for at in spans:
            if t == STEPS - 1:
                adjoint = state_ref[:, at] - cells_ref[STATE : 2 * STATE, at]
            else:
                adjoint = adj_ref[:, at]
            high, low = halves(TIME_STEP * adjoint)
            through = dot(wb, jnp.concatenate([high, high, low], axis=0)) * slope_ref[t, :, at]
            high, low = halves(through)
            both = dot(wt, high)
            both = both[: 2 * STATE] + both[2 * STATE :] + dot(wt[: 2 * STATE], low)
            adj_ref[:, at] = adjoint + both[:STATE]
            gained = both[STATE:]
            grad_ref[:, at] = gained if t == STEPS - 1 else grad_ref[:, at] + gained
    first_owner = jnp.max(place_ref[STEPS + 1 : STEPS + 2, 0:LANES]).astype(jnp.int32)
    total = jnp.zeros((FIELDS, cp), f32)
    place = iota((FIELDS, cp), 1)
    for m in range(nb):
        owner = lax.rem(first_owner + m, nb)
        at = pl.ds(m * cp, cp)
        count = arrived_ref[owner, 0:1, COUNT_LANE : COUNT_LANE + 1]
        product = grad_ref[:, at] * pattern_ref[:, at]
        total = total + jnp.where(place.astype(f32) < count, product, 0.0)
    summed = jnp.sum(total, axis=1, keepdims=True)
    for m in range(nb):
        owner = lax.rem(first_owner + m, nb)
        at = pl.ds(m * cp, cp)
        out_ref[owner, 0:STATE, :] = jnp.where(place == cap, summed, state_ref[:, at])
        out_ref[owner, STATE : 2 * STATE, :] = grad_ref[:, at]


def advance_call(nb, cap, cp, arrived, prepared):
    cells, place, inverse, dft, turn, amps, wx, wo, wt, wb = prepared
    length = nb * cp
    lc = 512
    vmem = pl.BlockSpec(memory_space=pltpu.VMEM)
    return pl.pallas_call(
        functools.partial(advance_kernel, nb, cap, cp, lc),
        in_specs=[vmem] * 11,
        out_shape=jax.ShapeDtypeStruct((nb, 2 * STATE, cp), f32),
        scratch_shapes=[
            pltpu.VMEM((LON_OUTER, FIELDS, LANES), f32),
            pltpu.VMEM((FIELDS, length), f32),
            pltpu.VMEM((3 * FIELDS, length), bf16),
            pltpu.VMEM((STEPS, 16, length), bf16),
            pltpu.VMEM((STATE, length), f32),
            pltpu.VMEM((STEPS, UNITS, length), f32),
            pltpu.VMEM((STATE, length), f32),
            pltpu.VMEM((FIELDS, length), f32),
        ],
        compiler_params=pltpu.CompilerParams(vmem_limit_bytes=VMEM_LIMIT),
        name="advance",
    )(arrived, inverse, dft, turn, amps, cells, place, wx, wo, wt, wb)


def owned_kernel(nb, cap, cp, slot_ref, received_ref, final_ref, grad_ref):
    per_row = cp // LANES
    for q in range(slot_ref.shape[1] // LANES):
        at = pl.ds(q * LANES, LANES)
        slot = slot_ref[:, at]
        row = ((slot.astype(f32) + 0.5) * (1.0 / cap)).astype(jnp.int32)
        place = slot - row * cap
        piece = row * per_row + place // LANES

        def load(i):
            return received_ref[i // per_row, :, pl.ds(i % per_row * LANES, LANES)]

        found = pick((nb * per_row, load), piece, place % LANES, 2 * STATE)
        final_ref[:, at] = found[:STATE]
        grad_ref[:, at] = found[STATE:]


def owned_call(nb, cap, cp, owner_slot, received):
    mean = owner_slot.shape[1]
    return pl.pallas_call(
        functools.partial(owned_kernel, nb, cap, cp),
        out_shape=[
            jax.ShapeDtypeStruct((STATE, mean), f32),
            jax.ShapeDtypeStruct((FIELDS, mean), f32),
        ],
        compiler_params=pltpu.CompilerParams(vmem_limit_bytes=VMEM_LIMIT),
        name="owned",
    )(owner_slot, received)


def body(
    spectra,
    pair_slot,
    land_column,
    owner_map,
    owner_slot,
    state_start,
    targets,
    amplitudes,
    weight_in,
    weight_out,
):
    nb = lax.axis_size("fld")
    ndev = lax.axis_size("band") * nb
    pc = spectra.shape[0]
    cap = ROW_MAX // nb
    cp = -(-cap // LANES) * LANES
    coeffs = fourier_call(nb, pc, cap, pair_slot, owner_slot, spectra)
    arrived = lax.all_to_all(coeffs, "fld", split_axis=0, concat_axis=0, tiled=True)
    prepared = prepare_call(
        nb, pc, cp, pair_slot, owner_map, land_column, state_start, targets,
        amplitudes[None, :], jnp.transpose(weight_in), weight_out,
    )
    outbound = advance_call(nb, cap, cp, arrived, prepared)
    received = lax.all_to_all(outbound, "fld", split_axis=0, concat_axis=0, tiled=True)
    total = jnp.sum(received[:, :FIELDS, cap], axis=0)
    bands = lax.axis_size("band")
    step = 1
    while step < bands:
        total = total + lax.ppermute(total, "band", [(i, i ^ step) for i in range(bands)])
        step *= 2
    final_state, param_grad = owned_call(nb, cap, cp, owner_slot, received)
    return (final_state, param_grad, total / math.sqrt(ndev * ROW_MEAN))


def solution(mesh):
    return jax.shard_map(
        body,
        mesh=mesh,
        in_specs=(
            P("fld", None, None),
            P(),
            P(("band", "fld"), None),
            P(("band", "fld"), None),
            P(("band", "fld"), None),
            P(None, ("band", "fld"), None),
            P(None, ("band", "fld"), None),
            P(),
            P(),
            P(),
        ),
        out_specs=(P(None, ("band", "fld")), P(None, ("band", "fld")), P()),
        check_vma=False,
    )
```

```python
import functools
import math

import jax
import jax.numpy as jnp
from jax import lax
from jax.experimental import pallas as pl
from jax.experimental.pallas import tpu as pltpu
from jax.sharding import PartitionSpec as P

FIELDS = 16
STATE = 16
UNITS = 256
WAVES = 960
LONS = 2048
LATS = 1024
STEPS = 4
ROW_MEAN = 640
COEFS = 961
ROW_MAX = 1920
PAIRS = 480
TIME_STEP = 0.25

LANES = 128
HALF = LANES // 2
COUNT_LANE = HALF - 1
COEF_PAD = 1024
COEF_TILES = COEF_PAD // LANES
LAST = COEFS - (COEF_TILES - 1) * LANES
EARLY = (WAVES - PAIRS + 1) // LANES
LON_OUTER = LONS // LANES
WAVE_INNER = 16
VMEM_LIMIT = 60 * 1024 * 1024

f32 = jnp.float32
bf16 = jnp.bfloat16


def iota(shape, dim):
    return lax.broadcasted_iota(jnp.int32, shape, dim)


def sincos_turns(turns):
    part = turns - jnp.round(turns)
    quarter = jnp.round(4.0 * part)
    x = (part - 0.25 * quarter) * (2.0 * math.pi)
    y = x * x
    sine = x * (1.0 + y * (-1.0 / 6 + y * (1.0 / 120 + y * (-1.0 / 5040 + y * (1.0 / 362880)))))
    cosine = 1.0 + y * (-0.5 + y * (1.0 / 24 + y * (-1.0 / 720 + y * (1.0 / 40320))))
    swap = jnp.abs(quarter) == 1.0
    low_sine = jnp.where(swap, cosine, sine)
    low_cosine = jnp.where(swap, sine, cosine)
    sine_flip = (quarter == -1.0) | (jnp.abs(quarter) == 2.0)
    cosine_flip = (quarter == 1.0) | (jnp.abs(quarter) == 2.0)
    return jnp.where(sine_flip, -low_sine, low_sine), jnp.where(cosine_flip, -low_cosine, low_cosine)


def halves(x):
    high = x.astype(bf16)
    return high, (x - high.astype(f32)).astype(bf16)


def on_chip(x):
    return pltpu.with_memory_space_constraint(x, pltpu.VMEM)


def dot(a, b):
    return jnp.dot(a, b, preferred_element_type=f32)


def dot_last(a, b):
    return lax.dot_general(a, b, (((1,), (1,)), ((), ())), preferred_element_type=f32)


def pick(pieces, piece_at, lane_at, rows):
    count, load = pieces
    lane_full = jnp.broadcast_to(lane_at, (rows, LANES))
    total = None
    for i in range(count):
        got = jnp.take_along_axis(load(i), lane_full, axis=1)
        total = got if total is None else jnp.where(piece_at == i, got, total)
    return total


def fourier_kernel(nb, pc, cap, gc, pairs_ref, slot_ref, spec_ref, out_ref, buf, tab, thr, lhs, tail, sem):
    lane = iota((nb, LANES), 1)
    rows = pc * gc
    groups = 2 * FIELDS // gc
    copies = []
    for k in range(groups):
        at = pl.ds(k * gc, gc)
        copies.append(pltpu.make_async_copy(spec_ref.at[:, at, :], buf.at[:, at, :], sem.at[k]))
        copies[k].start()
    band = lax.axis_index("band")
    first = lax.axis_index("fld") * pc
    odd = (2 * (band * nb + iota((nb, LANES), 0)) + 1).astype(f32) * (1.0 / (4 * LATS))
    for t in range(COEF_TILES):
        column = lane + t * LANES
        if t == COEF_TILES - 1:
            column = jnp.where(lane < LAST, column, lane + EARLY * LANES)
        sine, cosine = sincos_turns(column.astype(f32) * odd)
        high, low = halves(jnp.concatenate([cosine, sine], axis=0))
        at = pl.ds(t * LANES, LANES)
        tab[0 : 2 * nb, at] = high
        tab[2 * nb : 4 * nb, at] = low
    pieces = -(-rows // LANES)
    per_piece = LANES // gc
    sine1, cosine1 = sincos_turns(odd)
    factors = []
    for i in range(pieces):
        row = jnp.zeros((nb, LANES), f32)
        for s in range(i * per_piece, min((i + 1) * per_piece, pc)):
            pair = pairs_ref[first + s]
            row = jnp.where(lane // gc == s - i * per_piece, pair.astype(f32), row)
            thr[s * gc : (s + 1) * gc, :] = jnp.full((gc, LANES), WAVES - pair, jnp.int32)
        sine, cosine = sincos_turns(row * odd)
        is_odd = row - 2.0 * jnp.floor(row * 0.5) == 1.0
        factors.append(
            (
                jnp.where(is_odd, sine, cosine),
                jnp.where(is_odd, cosine, -sine),
                jnp.where(is_odd, cosine1, -sine1),
                jnp.where(is_odd, sine1, cosine1),
            )
        )
    wide = iota((rows, LANES), 1)
    for k in range(groups):
        copies[k].wait()
        base = k * rows
        here = slice(base, base + rows)
        early = None
        for t in range(COEF_TILES):
            at = pl.ds(t * LANES, LANES)
            if t < COEF_TILES - 1:
                x = buf[:, k * gc : (k + 1) * gc, at].reshape(rows, LANES)
            else:
                x = buf[:, k * gc : (k + 1) * gc, t * LANES : COEFS].reshape(rows, LAST)
                x = jnp.concatenate([x, jnp.zeros((rows, LANES - LAST), f32)], axis=1)
            high = x.astype(bf16)
            whole = high.astype(f32)
            rest = x - whole
            lhs[0, here, at] = high
            lhs[1, here, at] = rest.astype(bf16)
            if t == EARLY:
                early = whole, rest
            if t > EARLY:
                column = wide + t * LANES
                if t == COEF_TILES - 1:
                    column = jnp.where(wide < LAST, column, wide + EARLY * LANES)
                    whole = jnp.where(wide < LAST, whole, early[0])
                    rest = jnp.where(wide < LAST, rest, early[1])
                second = column >= thr[...]
                at = pl.ds((t - EARLY - 1) * LANES, LANES)
                tail[0, here, at] = jnp.where(second, whole, 0.0).astype(bf16)
                tail[1, here, at] = jnp.where(second, rest, 0.0).astype(bf16)
        end = slice((EARLY + 1) * LANES, COEF_PAD)
        everything = contract(lhs[0, here, :], tab[...]) + contract(lhs[1, here, :], tab[...])
        shifted = contract(tail[0, here, :], tab[:, end]) + contract(tail[1, here, :], tab[:, end])
        everything = everything[: 2 * nb] + everything[2 * nb :]
        shifted = shifted[: 2 * nb] + shifted[2 * nb :]
        pad = [(0, 0), (0, pieces * LANES - rows)]
        first_part, shifted = jnp.pad(everything - shifted, pad), jnp.pad(shifted, pad)
        waves = []
        for i, (alpha, beta, gamma, delta) in enumerate(factors):
            at = slice(i * LANES, (i + 1) * LANES)
            waves.append(alpha * first_part[:nb, at] + beta * first_part[nb:, at])
            waves.append(gamma * shifted[:nb, at] + delta * shifted[nb:, at])
        for g in range(gc):
            source = (iota((1, LANES), 1) % HALF) * gc + g
            piece_at = 2 * (source // LANES) + iota((1, LANES), 1) // HALF
            value = pick((2 * pieces, lambda i: waves[i]), piece_at, source % LANES, nb)
            value = jnp.where(lane % HALF < pc, value, 0.0)
            if k == 0 and g == 0:
                slot = jnp.broadcast_to(slot_ref[...], (nb, slot_ref.shape[1]))
                below = iota((nb, slot_ref.shape[1]), 0) * cap
                inside = (slot >= below) & (slot < below + cap)
                count = jnp.sum(jnp.where(inside, 1.0, 0.0), axis=1, keepdims=True)
                value = jnp.where(lane == COUNT_LANE, count, value)
            out_ref[:, k * gc + g, :] = value


def contract(values, table):
    return jnp.transpose(dot_last(values, table))


def fourier_call(nb, pc, cap, pair_slot, owner_slot, spectra):
    gc = 8
    rows = 2 * FIELDS * pc
    return pl.pallas_call(
        functools.partial(fourier_kernel, nb, pc, cap, gc),
        in_specs=[
            pl.BlockSpec(memory_space=pltpu.SMEM),
            pl.BlockSpec(memory_space=pltpu.VMEM),
            pl.BlockSpec(memory_space=pl.ANY),
        ],
        out_shape=jax.ShapeDtypeStruct((nb, 2 * FIELDS, LANES), f32),
        scratch_shapes=[
            pltpu.VMEM(spectra.shape, f32),
            pltpu.VMEM((4 * nb, COEF_PAD), bf16),
            pltpu.VMEM((pc * gc, LANES), jnp.int32),
            pltpu.VMEM((2, rows, COEF_PAD), bf16),
            pltpu.VMEM((2, rows, COEF_PAD - (EARLY + 1) * LANES), bf16),
            pltpu.SemaphoreType.DMA((2 * FIELDS // gc,)),
        ],
        compiler_params=pltpu.CompilerParams(vmem_limit_bytes=VMEM_LIMIT),
        name="fourier",
    )(pair_slot, owner_slot, spectra)


def prepare_kernel(nb, pc, cp, pairs_ref, owner_ref, land_ref, state_ref, target_ref, amp_ref, win_ref, wout_ref,
                   cells_ref, place_ref, inverse_ref, dft_ref, turn_ref, amps_ref,
                   wx_ref, wo_ref, wt_ref, wb_ref):
    lane = iota((1, LANES), 1)
    source_pieces = ROW_MAX // LANES
    row = lax.axis_index("band") * nb + lax.axis_index("fld")
    odd = (2 * row + 1).astype(f32) * (0.5 / (2 * LATS))
    sin_colat = sincos_turns(jnp.full((8, LANES), 1.0, f32) * odd)[0]
    joined = 2 * STATE
    for m in range(nb):
        for q in range(cp // LANES):
            source = nb * (q * LANES + lane) + m
            first = nb * q
            count = min(nb, source_pieces - first)
            at = pl.ds(m * cp + q * LANES, LANES)
            piece_at, lane_at = source // LANES - first, source % LANES

            def load(ref, i):
                return ref[:, 0, pl.ds((first + i) * LANES, LANES)]

            for k, ref in enumerate((state_ref, target_ref)):
                cells_ref[k * STATE : (k + 1) * STATE, at] = pick(
                    (count, functools.partial(load, ref)), piece_at, lane_at, STATE
                )

            def load_land(i):
                return jnp.broadcast_to(land_ref[:, pl.ds((first + i) * LANES, LANES)], (8, LANES))

            column = pick((count, load_land), piece_at, lane_at, 8)
            hour = iota((8, LANES), 0).astype(f32)
            turns = column.astype(f32) * (1.0 / LONS) + hour * (1.0 / 24.0)
            forcing = jnp.maximum(sincos_turns(turns)[1], 0.0) * sin_colat
            rest = jnp.where(iota((8, LANES), 0) == STEPS, column, owner_ref[0:1, 0:1]).astype(f32)
            place_ref[:, at] = jnp.where(iota((8, LANES), 0) < STEPS, forcing, rest)
    natural = iota((8, LANES), 0) * LANES + iota((8, LANES), 1)
    wave = (natural % HALF) * WAVE_INNER + natural // HALF
    pair = jnp.minimum(wave, WAVES - 1 - wave)
    totals = [jnp.where(wave >= PAIRS, HALF, 0)] + [jnp.zeros((8, LANES), jnp.int32)] * 3
    for i in range(PAIRS):
        arrives = i // pc * LANES + i % pc
        totals[i % 4] = jnp.where(pair == pairs_ref[i], totals[i % 4] + arrives, totals[i % 4])
    inverse_ref[...] = totals[0] + totals[1] + totals[2] + totals[3]
    a = iota((HALF, LANES), 0)
    sine, cosine = sincos_turns((a * iota((HALF, LANES), 1)).astype(f32) * (1.0 / LANES))
    table = jnp.concatenate(
        [jnp.concatenate([cosine, sine], axis=1), jnp.concatenate([-sine, cosine], axis=1)], axis=0
    )
    high, low = halves(table)
    dft_ref[0:LANES, :] = high
    dft_ref[LANES : 2 * LANES, :] = high
    dft_ref[2 * LANES : 3 * LANES, :] = low
    b = iota((WAVE_INNER, LANES), 0)
    sine, cosine = sincos_turns((b * iota((WAVE_INNER, LANES), 1)).astype(f32) * (1.0 / LONS))
    turn_ref[0:WAVE_INNER, :] = cosine
    turn_ref[WAVE_INNER : 2 * WAVE_INNER, :] = sine
    amp = jnp.broadcast_to(amp_ref[...], (FIELDS, FIELDS))
    diagonal = iota((FIELDS, FIELDS), 0) == iota((FIELDS, FIELDS), 1)
    amps_ref[...] = jnp.broadcast_to(
        jnp.sum(jnp.where(diagonal, amp, 0.0), axis=1, keepdims=True), (FIELDS, LANES)
    )
    turned = win_ref[...]
    wout = wout_ref[...]
    high, low = halves(turned[:joined])
    wt_ref[0:joined, :] = high
    wt_ref[joined : 2 * joined, :] = low
    high, low = halves(jnp.transpose(turned))
    s, p = slice(0, STATE), slice(STATE, joined)
    tail = jnp.where(iota((UNITS, STATE), 1) == 0, high[:, joined:].astype(f32), 0.0)
    tail = jnp.where(iota((UNITS, STATE), 1) == 1, low[:, joined:].astype(f32), tail)
    tail = jnp.where(iota((UNITS, STATE), 1) == 2, high[:, joined:].astype(f32), tail)
    hf, lf = high.astype(f32), low.astype(f32)
    wx_ref[...] = jnp.concatenate(
        [hf[:, s], lf[:, s], hf[:, s], hf[:, p], lf[:, p], hf[:, p], tail], axis=1
    ).astype(bf16)
    high, low = halves(wout)
    wo_ref[0:STATE, :] = high
    wo_ref[STATE : 2 * STATE, :] = low
    turned = jnp.transpose(wout)
    high, low = halves(turned)
    hf, lf = high.astype(f32), low.astype(f32)
    wb_ref[...] = jnp.concatenate([hf, lf, hf], axis=1).astype(bf16)


def prepare_call(nb, pc, cp, *arrays):
    length = nb * cp
    shapes = [
        ((2 * STATE, length), f32),
        ((8, length), f32),
        ((8, LANES), jnp.int32),
        ((3 * LANES, 2 * LANES), bf16),
        ((2 * WAVE_INNER, LANES), f32),
        ((FIELDS, LANES), f32),
        ((UNITS, 6 * STATE + 16), bf16),
        ((2 * STATE, UNITS), bf16),
        ((4 * STATE, UNITS), bf16),
        ((UNITS, 3 * STATE), bf16),
    ]
    vmem = pl.BlockSpec(memory_space=pltpu.VMEM)
    return pl.pallas_call(
        functools.partial(prepare_kernel, nb, pc, cp),
        in_specs=[pl.BlockSpec(memory_space=pltpu.SMEM)] + [vmem] * (len(arrays) - 1),
        out_shape=[pltpu.VMEM(*s) for s in shapes],
        compiler_params=pltpu.CompilerParams(vmem_limit_bytes=VMEM_LIMIT),
        name="prepare",
    )(*arrays)


def advance_kernel(nb, cap, cp, lc, arrived_ref, inverse_ref, dft_ref, turn_ref, amps_ref, cells_ref,
                   place_ref, wx_ref, wo_ref, wt_ref, wb_ref, out_ref,
                   grid_ref, pattern_ref, param_ref, force_ref, state_ref, slope_ref, adj_ref, grad_ref):
    length = nb * cp
    lane = iota((1, LANES), 1)
    rows = iota((FIELDS, LANES), 1)
    low_half = rows < HALF
    blocks = []
    for q in range(WAVE_INNER // 2):
        natural = lane + q * LANES
        wave = (natural % HALF) * WAVE_INNER + natural // HALF
        at = inverse_ref[q : q + 1, :]
        x = pick((nb, lambda i: arrived_ref[i]), at // LANES, at % LANES, 2 * FIELDS)
        x = jnp.where(wave < WAVES, x * jnp.where(wave == 0, 1.0, 2.0), 0.0)
        real, imag = x[:FIELDS], x[FIELDS:]
        blocks.append(jnp.where(low_half, real, pltpu.roll(imag, HALF, 1)))
        blocks.append(jnp.where(low_half, pltpu.roll(real, HALF, 1), imag))
    coeffs = jnp.concatenate(blocks, axis=0)
    high, low = halves(coeffs)
    partial = dot(high, dft_ref[0:LANES]) + dot(low, dft_ref[0:LANES]) + dot(high, dft_ref[2 * LANES : 3 * LANES])
    reals, imags = [], []
    for b in range(WAVE_INNER):
        y_real = partial[b * FIELDS : (b + 1) * FIELDS, :LANES]
        y_imag = partial[b * FIELDS : (b + 1) * FIELDS, LANES:]
        cosine, sine = turn_ref[b : b + 1, :], turn_ref[WAVE_INNER + b : WAVE_INNER + b + 1, :]
        reals.append(y_real * cosine - y_imag * sine)
        imags.append(y_real * sine + y_imag * cosine)
    half = WAVE_INNER // 2
    sums = [reals[b] + reals[WAVE_INNER - b] for b in range(1, half)]
    gaps = [imags[b] - imags[WAVE_INNER - b] for b in range(1, half)]
    for c in range(half + 1):
        even = reals[0] + reals[half] if c % 2 == 0 else reals[0] - reals[half]
        odd = None
        for b in range(1, half):
            turn = 2.0 * math.pi * (b * c % WAVE_INNER) / WAVE_INNER
            even = even + math.cos(turn) * sums[b - 1]
            term = math.sin(turn) * gaps[b - 1]
            odd = term if odd is None else odd + term
        grid_ref[c] = even - odd
        if 0 < c < half:
            grid_ref[WAVE_INNER - c] = even + odd
    amps = amps_ref[...]
    for q in range(length // LANES):
        at = pl.ds(q * LANES, LANES)
        column = place_ref[STEPS : STEPS + 1, at].astype(jnp.int32)
        found = pick((LON_OUTER, lambda i: grid_ref[i]), column // LANES, column % LANES, FIELDS)
        pattern_ref[:, at] = found
        high, low = halves(amps * found)
        param_ref[0:FIELDS, at] = high
        param_ref[FIELDS : 2 * FIELDS, at] = high
        param_ref[2 * FIELDS : 3 * FIELDS, at] = low
        row16 = iota((16, LANES), 0)
        for t in range(STEPS):
            force = place_ref[t : t + 1, at]
            force_high = force.astype(bf16).astype(f32)
            packed = jnp.where(row16 < 2, force_high, jnp.where(row16 == 2, force - force_high, 0.0))
            force_ref[t, :, at] = packed.astype(bf16)
    state_ref[...] = cells_ref[0:STATE, :]
    spans = [pl.ds(i * lc, lc) for i in range(length // lc)]
    wx, wo, wt, wb = wx_ref[...], wo_ref[...], wt_ref[...], wb_ref[...]
    for t in range(STEPS):
        for at in spans:
            state = state_ref[:, at]
            high, low = halves(state)
            joined = jnp.concatenate([high, high, low, param_ref[:, at], force_ref[t, :, at]], axis=0)
            hidden = jnp.tanh(dot(wx, joined))
            slope_ref[t, :, at] = 1.0 - hidden * hidden
            high, low = halves(hidden)
            moved = dot(wo, high)
            moved = moved[:STATE] + moved[STATE:] + dot(wo[:STATE], low)
            state_ref[:, at] = state + TIME_STEP * moved
    for t in reversed(range(STEPS)):
        for at in spans:
            if t == STEPS - 1:
                adjoint = state_ref[:, at] - cells_ref[STATE : 2 * STATE, at]
            else:
                adjoint = adj_ref[:, at]
            high, low = halves(TIME_STEP * adjoint)
            through = dot(wb, jnp.concatenate([high, high, low], axis=0)) * slope_ref[t, :, at]
            high, low = halves(through)
            both = dot(wt, high)
            both = both[: 2 * STATE] + both[2 * STATE :] + dot(wt[: 2 * STATE], low)
            adj_ref[:, at] = adjoint + both[:STATE]
            gained = both[STATE:]
            grad_ref[:, at] = gained if t == STEPS - 1 else grad_ref[:, at] + gained
    first_owner = jnp.max(place_ref[STEPS + 1 : STEPS + 2, 0:LANES]).astype(jnp.int32)
    total = jnp.zeros((FIELDS, cp), f32)
    place = iota((FIELDS, cp), 1)
    for m in range(nb):
        owner = lax.rem(first_owner + m, nb)
        at = pl.ds(m * cp, cp)
        count = arrived_ref[owner, 0:1, COUNT_LANE : COUNT_LANE + 1]
        product = grad_ref[:, at] * pattern_ref[:, at]
        total = total + jnp.where(place.astype(f32) < count, product, 0.0)
    summed = jnp.sum(total, axis=1, keepdims=True)
    for m in range(nb):
        owner = lax.rem(first_owner + m, nb)
        at = pl.ds(m * cp, cp)
        out_ref[owner, 0:STATE, :] = jnp.where(place == cap, summed, state_ref[:, at])
        out_ref[owner, STATE : 2 * STATE, :] = grad_ref[:, at]


def advance_call(nb, cap, cp, arrived, prepared):
    cells, place, inverse, dft, turn, amps, wx, wo, wt, wb = prepared
    length = nb * cp
    lc = 256
    vmem = pl.BlockSpec(memory_space=pltpu.VMEM)
    return pl.pallas_call(
        functools.partial(advance_kernel, nb, cap, cp, lc),
        in_specs=[vmem] * 11,
        out_shape=jax.ShapeDtypeStruct((nb, 2 * STATE, cp), f32),
        scratch_shapes=[
            pltpu.VMEM((LON_OUTER, FIELDS, LANES), f32),
            pltpu.VMEM((FIELDS, length), f32),
            pltpu.VMEM((3 * FIELDS, length), bf16),
            pltpu.VMEM((STEPS, 16, length), bf16),
            pltpu.VMEM((STATE, length), f32),
            pltpu.VMEM((STEPS, UNITS, length), f32),
            pltpu.VMEM((STATE, length), f32),
            pltpu.VMEM((FIELDS, length), f32),
        ],
        compiler_params=pltpu.CompilerParams(vmem_limit_bytes=VMEM_LIMIT),
        name="advance",
    )(*(on_chip(x) for x in (arrived, inverse, dft, turn, amps, cells, place, wx, wo, wt, wb)))


def owned_kernel(nb, cap, cp, slot_ref, received_ref, final_ref, grad_ref):
    per_row = cp // LANES
    for q in range(slot_ref.shape[1] // LANES):
        at = pl.ds(q * LANES, LANES)
        slot = slot_ref[:, at]
        row = ((slot.astype(f32) + 0.5) * (1.0 / cap)).astype(jnp.int32)
        place = slot - row * cap
        piece = row * per_row + place // LANES

        def load(i):
            return received_ref[i // per_row, :, pl.ds(i % per_row * LANES, LANES)]

        found = pick((nb * per_row, load), piece, place % LANES, 2 * STATE)
        final_ref[:, at] = found[:STATE]
        grad_ref[:, at] = found[STATE:]


def owned_call(nb, cap, cp, owner_slot, received):
    mean = owner_slot.shape[1]
    return pl.pallas_call(
        functools.partial(owned_kernel, nb, cap, cp),
        out_shape=[
            jax.ShapeDtypeStruct((STATE, mean), f32),
            jax.ShapeDtypeStruct((FIELDS, mean), f32),
        ],
        compiler_params=pltpu.CompilerParams(vmem_limit_bytes=VMEM_LIMIT),
        name="owned",
    )(owner_slot, on_chip(received))


def body(
    spectra,
    pair_slot,
    land_column,
    owner_map,
    owner_slot,
    state_start,
    targets,
    amplitudes,
    weight_in,
    weight_out,
):
    nb = lax.axis_size("fld")
    ndev = lax.axis_size("band") * nb
    pc = spectra.shape[0]
    cap = ROW_MAX // nb
    cp = -(-cap // LANES) * LANES
    coeffs = fourier_call(nb, pc, cap, pair_slot, owner_slot, spectra)
    arrived = lax.all_to_all(coeffs, "fld", split_axis=0, concat_axis=0, tiled=True)
    prepared = prepare_call(
        nb, pc, cp, pair_slot, owner_map, land_column, state_start, targets,
        amplitudes[None, :], jnp.transpose(weight_in), weight_out,
    )
    outbound = advance_call(nb, cap, cp, arrived, prepared)
    received = lax.all_to_all(outbound, "fld", split_axis=0, concat_axis=0, tiled=True)
    total = jnp.sum(received[:, :FIELDS, cap], axis=0)
    bands = lax.axis_size("band")
    step = 1
    while step < bands:
        total = total + lax.ppermute(total, "band", [(i, i ^ step) for i in range(bands)])
        step *= 2
    final_state, param_grad = owned_call(nb, cap, cp, owner_slot, received)
    return (final_state, param_grad, total / math.sqrt(ndev * ROW_MEAN))


def solution(mesh):
    return jax.shard_map(
        body,
        mesh=mesh,
        in_specs=(
            P("fld", None, None),
            P(),
            P(("band", "fld"), None),
            P(("band", "fld"), None),
            P(("band", "fld"), None),
            P(None, ("band", "fld"), None),
            P(None, ("band", "fld"), None),
            P(),
            P(),
            P(),
        ),
        out_specs=(P(None, ("band", "fld")), P(None, ("band", "fld")), P()),
        check_vma=False,
    )
```
